128 devices in a mesh: grp: 4 (over x), blk: 32 (over z, y, core).
Axes of the slice: x: 4, y: 4, z: 4, core: 2. Of those that a mesh axis runs over, the one named last changes fastest.
Arguments:
- activations: bfloat16 [131072, 3072], P(('grp', 'blk')), may hold values from -6 to 6
- out_grads: bfloat16 [131072, 3072], P(('grp', 'blk')), may hold values from -6 to 6
- proj_act: bfloat16 [3072, 128], replicated, may hold values from -1 to 1
- proj_out: bfloat16 [3072, 256], replicated, may hold values from -0.109375 to 0.109375
Outputs:
- scores: float32 [2048, 512], P(('grp', 'blk'))
The draws below stay inside these ranges and needn't reach their ends.
All inputs are finite; a program needn't handle non-finite values.
Results may differ from the reference program's by a relative error of at most 0.0012.
Values may be sent and summed in bfloat16 or wider, within the bound.
No kernel may reach another device: no remote copies, remote signals or barrier semaphores. Data moves between devices by JAX's collectives and lax.ppermute only.
A program may use at most 64 MiB of HBM per device.

```python
import math
import jax
import jax.numpy as jnp
from jax import lax

D = 3072
RA = 128
RB = 256
SEQ = 64
ITERS = 4
EX_DEV = 16
GROUPS = 4
BLOCKS = 32
GROUP_EX = 512
EXAMPLES = 2048
TOKENS = 131072
COORDS = 32768
COORD_BLK = 1024


def draw_proj_act(key, part):
    base = jnp.clip(jax.random.normal(jax.random.fold_in(key, 11), (D, RA), jnp.float32), -6.0, 6.0)
    ladder = jnp.arange(RA).astype(jnp.float32) / RA
    jitter = jax.random.uniform(jax.random.fold_in(key, 12), (RA,), jnp.float32, -0.4, 0.4)
    column = jnp.exp(ladder * math.log(3.0) + jitter)
    values = jnp.clip(base * column / math.sqrt(D), -1.0, 1.0)
    return values.astype(jnp.bfloat16)


def level_of(key, shape, pieces, smallest, top_value):
    def one(axis_at, blocks):
        steps = jax.random.uniform(jax.random.fold_in(jax.random.fold_in(key, 6), axis_at), (blocks,), jnp.float32, smallest / len(pieces), top_value / len(pieces))
        return jnp.repeat(jnp.exp(steps), shape[axis_at] // blocks).reshape((-1,) + (1,) * (len(shape) - axis_at - 1))

    loudness = one(*pieces[0])
    for cut in pieces[1:]:
        loudness = loudness * one(*cut)
    return loudness


def normal_values(own_key, shape, deviation, limit, cuts=(), held_as=jnp.bfloat16):
    values = jax.random.normal(own_key, shape, jnp.float32) * deviation
    if len(cuts) > 0:
        values = level_of(own_key, shape, cuts, -0.22, 0.18) * values
    return jnp.clip(values, min=-limit, max=limit).astype(held_as)


def setup_inputs(seed: int = 0) -> dict:
    splits = jax.random.split(jax.random.key(seed), 5)
    return {
        "activations": normal_values(splits[0], (TOKENS, D), 1.0, 6.0, ((0, 128),)),
        "out_grads": normal_values(splits[1], (TOKENS, D), 1.0, 6.0, ((0, 128),)),
        "proj_act": draw_proj_act(jax.random.fold_in(splits[4], 71), 0),
        "proj_out": normal_values(splits[3], (D, RB), D ** -0.5, 0.109375),
    }


damping_rate = 0.5
power_steps = 3

def top_estimate(gram_sum):
    width = gram_sum.shape[0]
    vector = jnp.full((width,), 1.0 / math.sqrt(width), jnp.float32)
    top = jnp.float32(1.0)
    for step in range(power_steps):
        image = jnp.dot(gram_sum, vector, precision=lax.Precision.HIGHEST)
        top = jnp.sqrt(jnp.sum(image * image) + 1e-06)
        vector = image / top
    return top

def chebyshev(gram_sum, damping, right_side):
    radius = top_estimate(gram_sum)
    center = damping + radius

    def operate(field):
        return jnp.dot(gram_sum, field, precision=lax.Precision.HIGHEST) + damping * field
    stride = 1.0 / center
    direction = right_side
    solution = stride * direction
    residual = right_side - stride * operate(direction)
    for sweep in range(1, ITERS):
        if sweep == 1:
            momentum = 0.5 * (radius * stride) ** 2
        else:
            momentum = (0.5 * radius * stride) ** 2
        stride = 1.0 / (center - momentum / stride)
        direction = residual + momentum * direction
        solution = solution + stride * direction
        if sweep + 1 < ITERS:
            residual = residual - stride * operate(direction)
    return solution

def reference(activations, out_grads, proj_act, proj_out):
    act_low = jnp.dot(activations, proj_act, preferred_element_type=jnp.float32).astype(jnp.bfloat16)
    grad_low = jnp.dot(out_grads, proj_out, preferred_element_type=jnp.float32).astype(jnp.bfloat16)
    features = jnp.einsum('etr,ets->ers', act_low.reshape(EXAMPLES, SEQ, RA).astype(jnp.float32), grad_low.reshape(EXAMPLES, SEQ, RB).astype(jnp.float32), precision=lax.Precision.HIGHEST)
    features = features.astype(jnp.bfloat16).reshape(EXAMPLES, COORDS)
    widened = features.astype(jnp.float32)
    total = jnp.sum(widened * widened)
    damping = damping_rate * total / COORDS
    grouped = features.reshape(GROUPS, GROUP_EX, BLOCKS, COORD_BLK)

    def one_block(running, block_rows):
        wide_rows = block_rows.astype(jnp.float32)
        gram_sum = jnp.einsum('gec,ged->cd', wide_rows, wide_rows, precision=lax.Precision.HIGHEST)

        def per_group(rows):
            solved = chebyshev(gram_sum, damping, rows.T)
            solved = lax.optimization_barrier(solved.astype(jnp.bfloat16)).astype(jnp.float32)
            return jnp.dot(rows, solved, precision=lax.Precision.HIGHEST)
        return (running + jax.vmap(per_group)(wide_rows), None)
    start_sum = jnp.zeros((GROUPS, GROUP_EX, GROUP_EX), jnp.float32)
    running, _ = lax.scan(one_block, start_sum, jnp.moveaxis(grouped, 2, 0))
    return running.reshape(EXAMPLES, GROUP_EX) * float(EX_DEV * GROUPS)
```

```python
import functools

import jax
import jax.numpy as jnp
from jax import lax
from jax.experimental import pallas as pl
from jax.experimental.pallas import tpu as pltpu
from jax.sharding import Mesh
from jax.sharding import PartitionSpec as P

SEQ = 64
ITERS = 4
BLK = ("blk_0", "blk_1", "blk_2")
GRP_BLK = ("grp", "blk_0", "blk_1", "blk_2")
TILE = 128
PIECES = 9

damping_rate = 0.5
power_steps = 3


def mxu(a, b, dims):
    return lax.dot_general(a, b, (dims, ((), ())), preferred_element_type=jnp.float32)


def feature_kernel(
    act_ref, grad_ref, pa_ref, po_ref, out_ref, sum_ref, act_low, grad_low, feats, by_coord
):
    step = pl.program_id(0)
    steps = pl.num_programs(0)
    tokens = act_ref.shape[0]
    rows = pl.ds(pl.multiple_of(step * tokens, tokens), tokens)
    act_low[rows, :] = mxu(act_ref[...], pa_ref[...], ((1,), (0,))).astype(jnp.bfloat16)
    grad_low[rows, :] = mxu(grad_ref[...], po_ref[...], ((1,), (0,))).astype(jnp.bfloat16)
    blocks, examples, width = out_ref.shape
    per = width // grad_low.shape[1]
    cols = grad_low.shape[1]

    def eight(half):
        for e in range(8):
            at = pl.ds((half * 8 + e) * SEQ, SEQ)
            feats[e] = mxu(act_low[at, :], grad_low[at, :], ((0,), (0,)))
        turned = jnp.swapaxes(feats[...], 0, 1)
        turned = turned.reshape(blocks, per, 8, cols)
        for j in range(per):
            by_coord[:, half * 8 : half * 8 + 8, j * cols : (j + 1) * cols] = turned[:, j]

    @pl.when(step == steps // 2)
    def _():
        eight(0)

    @pl.when(step == steps - 1)
    def _():
        eight(1)
        acc = jnp.zeros((examples, width), jnp.float32)
        for k in range(blocks):
            low = by_coord[k].astype(jnp.bfloat16)
            out_ref[k] = low
            wide = low.astype(jnp.float32)
            acc = acc + wide * wide
        part = jnp.zeros((8, TILE), jnp.float32)
        for r in range(0, examples, 8):
            for c in range(0, width, TILE):
                part = part + acc[r : r + 8, c : c + TILE]
        sum_ref[...] = part


def features_of(activations, out_grads, proj_act, proj_out, blocks):
    arguments = (activations, out_grads, proj_act, proj_out)
    tokens, depth = activations.shape
    examples = tokens // SEQ
    ra, rb = proj_act.shape[1], proj_out.shape[1]
    width = ra * rb // blocks
    steps = 4
    size = tokens // steps
    return pl.pallas_call(
        feature_kernel,
        grid=(steps,),
        in_specs=[
            pl.BlockSpec((size, depth), lambda i: (i, 0)),
            pl.BlockSpec((size, depth), lambda i: (i, 0)),
            pl.BlockSpec((depth, ra), lambda i: (0, 0), pipeline_mode=pl.Buffered(1)),
            pl.BlockSpec((depth, rb), lambda i: (0, 0), pipeline_mode=pl.Buffered(1)),
        ],
        out_specs=[
            pl.BlockSpec((blocks, examples, width), lambda i: (0, 0, 0)),
            pl.BlockSpec((8, TILE), lambda i: (0, 0)),
        ],
        out_shape=[
            jax.ShapeDtypeStruct((blocks, examples, width), jnp.bfloat16),
            jax.ShapeDtypeStruct((8, TILE), jnp.float32),
        ],
        scratch_shapes=[
            pltpu.VMEM((tokens, ra), jnp.bfloat16),
            pltpu.VMEM((tokens, rb), jnp.bfloat16),
            pltpu.VMEM((8, ra, rb), jnp.float32),
            pltpu.VMEM((blocks, examples, width), jnp.float32),
        ],
        compiler_params=pltpu.CompilerParams(
            dimension_semantics=("arbitrary",), vmem_limit_bytes=32 << 20
        ),
        name="features",
    )(*(pltpu.with_memory_space_constraint(x, pltpu.HBM) for x in arguments))


def places(high):
    return (
        (0, 0),
        (0, 1),
        (1, 1),
        (0, 2),
        (0, 3),
        (1, 2),
        (1, 3),
        (0, 5),
        (high, high + 4),
    )


def gram_kernel(place_ref, rows_ref, own_ref, up_ref, two_ref, down_ref, parts):
    wide = 2 * TILE

    def columns(first, count):
        return rows_ref[:, first * TILE : (first + count) * TILE]

    for q in range(4):
        left = columns(2 * q, 2)
        near = mxu(left, columns(2 * q, 2), ((0,), (0,)))
        after = mxu(left, columns((2 * q + 2) % 8, 2), ((0,), (0,)))
        if q < 2:
            far = mxu(columns(2 * q, 1), columns(2 * q + 4, 2), ((0,), (0,)))
            last = (far[:, TILE:wide], far[:, :TILE])
        else:
            far = mxu(left, columns((2 * q + 5) % 8, 1), ((0,), (0,)))
            last = (far[:TILE], far[TILE:wide])
        pieces = (
            near[:TILE, :TILE],
            near[:TILE, TILE:],
            near[TILE:, TILE:],
            after[:TILE, :TILE],
            after[:TILE, TILE:],
            after[TILE:, :TILE],
            after[TILE:, TILE:],
        ) + last
        for n, piece in enumerate(pieces):
            parts[q, n] = piece
    place = place_ref[0]
    own_ref[...] = parts[place]
    for shift, ref in ((1, up_ref), (2, two_ref), (3, down_ref)):
        ref[...] = parts[lax.rem(place + shift, 4)].astype(jnp.bfloat16)


def gram_parts(place, rows):
    shape = (PIECES, TILE, TILE)
    return pl.pallas_call(
        gram_kernel,
        in_specs=[
            pl.BlockSpec(memory_space=pltpu.SMEM),
            pl.BlockSpec(memory_space=pltpu.VMEM),
        ],
        out_specs=[pl.BlockSpec(memory_space=pltpu.VMEM)] * 4,
        out_shape=[jax.ShapeDtypeStruct(shape, jnp.float32)]
        + [jax.ShapeDtypeStruct(shape, jnp.bfloat16)] * 3,
        scratch_shapes=[pltpu.VMEM((4,) + shape, jnp.float32)],
        compiler_params=pltpu.CompilerParams(vmem_limit_bytes=16 << 20),
        name="gram_parts",
    )(place, rows)


def solve_kernel(place_ref, total_ref, own_ref, one_ref, two_ref, three_ref, rows_ref, out_ref, gram):
    place = place_ref[0]
    for back, ref in ((0, own_ref), (1, one_ref), (2, two_ref), (3, three_ref)):
        quarter = lax.rem(place + 4 - back, 4)
        high = lax.div(quarter, 2)
        for n, (i, j) in enumerate(places(high)):
            piece = ref[n]
            row = pl.multiple_of(lax.rem(2 * quarter + i, 8) * TILE, TILE)
            col = pl.multiple_of(lax.rem(2 * quarter + j, 8) * TILE, TILE)
            gram[pl.ds(row, TILE), pl.ds(col, TILE)] = piece
            if n not in (0, 2):
                gram[pl.ds(col, TILE), pl.ds(row, TILE)] = piece.T
    width = gram.shape[0]
    turn = lax.broadcasted_iota(jnp.int32, (16, width), 0)
    vector = jnp.full((1, width), 1.0 / width**0.5, jnp.float32)
    for _ in range(power_steps):
        high = vector.astype(jnp.bfloat16).astype(jnp.float32)
        rest = vector - high
        mid = rest.astype(jnp.bfloat16).astype(jnp.float32)
        low = rest - mid
        three = jnp.where(turn == 0, high, jnp.where(turn == 1, mid, jnp.where(turn == 2, low, 0.0)))
        image = mxu(three.astype(jnp.bfloat16), gram[...], ((1,), (0,)))
        image = jnp.sum(image, axis=0, keepdims=True)
        radius = jnp.sqrt(jnp.sum(image * image, axis=1, keepdims=True) + 1e-06)
        vector = image / radius
    damping = total_ref[0] * damping_rate
    center = damping + radius

    rows = rows_ref[...]
    right_side = rows.astype(jnp.float32)

    def operate(field):
        return mxu(field.astype(jnp.bfloat16), gram[...], ((1,), (0,))) + damping * field

    stride = 1.0 / center
    direction = right_side
    solution = stride * direction
    residual = right_side - stride * operate(direction)
    for sweep in range(1, ITERS):
        if sweep == 1:
            momentum = 0.5 * (radius * stride) ** 2
        else:
            momentum = (0.5 * radius * stride) ** 2
        stride = 1.0 / (center - momentum / stride)
        direction = residual + momentum * direction
        solution = solution + stride * direction
        if sweep + 1 < ITERS:
            residual = residual - stride * operate(direction)
    out_ref[...] = mxu(rows, solution.astype(jnp.bfloat16), ((1,), (1,))).astype(out_ref.dtype)


def block_scores(place, mean_square, quarters, rows):
    vmem = pl.BlockSpec(memory_space=pltpu.VMEM)
    smem = pl.BlockSpec(memory_space=pltpu.SMEM)
    examples, width = rows.shape
    return pl.pallas_call(
        solve_kernel,
        in_specs=[smem, smem, vmem, vmem, vmem, vmem, vmem],
        out_specs=vmem,
        out_shape=jax.ShapeDtypeStruct((examples, examples), jnp.bfloat16),
        scratch_shapes=[pltpu.VMEM((width, width), jnp.bfloat16)],
        compiler_params=pltpu.CompilerParams(vmem_limit_bytes=32 << 20),
        name="solve",
    )(place, mean_square, *quarters, rows)


def shifted(value, axis, shift):
    size = lax.axis_size(axis)
    return lax.ppermute(value, axis, [(i, (i + shift) % size) for i in range(size)])


def sum_over(value, axis):
    size = lax.axis_size(axis)
    shift = 1
    while shift < size:
        value = value + shifted(value, axis, shift)
        shift *= 2
    return value


def shards(activations, out_grads, proj_act, proj_out):
    examples = activations.shape[0] // SEQ
    blocks = lax.axis_size(BLK)
    by_block, squares = features_of(activations, out_grads, proj_act, proj_out, blocks)
    arrived = lax.all_to_all(by_block, BLK, 0, 0, tiled=True)
    rows = arrived.reshape(blocks * examples, -1)
    width = rows.shape[1]

    total = squares
    for axis in ("grp", "blk_2"):
        total = sum_over(total, axis)
    rows, total = lax.optimization_barrier((rows, total))

    place = lax.axis_index("grp").astype(jnp.int32).reshape(1)
    own, up, two, down = gram_parts(place, rows)
    others = [shifted(part, "grp", shift) for shift, part in ((1, up), (2, two), (3, down))]
    total = sum_over(total, "blk_1")
    total, *others = lax.optimization_barrier((total, *others))
    quarter = own
    for part in others:
        quarter = quarter + part.astype(jnp.float32)
    quarter = quarter.astype(jnp.bfloat16)
    quarters = [quarter] + [shifted(quarter, "grp", shift) for shift in (1, 2, 3)]
    total = sum_over(total, "blk_0")
    mean_square = (jnp.sum(total) / (width * blocks)).reshape(1)
    term = block_scores(place, mean_square, quarters, rows)
    terms = lax.all_to_all(term.reshape(blocks, examples, -1), BLK, 0, 0, tiled=True)
    scores = jnp.sum(terms.astype(jnp.float32), axis=0)
    return scores * float(examples * lax.axis_size("grp"))


def solution(mesh):
    split = Mesh(
        mesh.devices.reshape(mesh.shape["grp"], 4, 4, 2), ("grp", "blk_0", "blk_1", "blk_2")
    )
    placed = (P(GRP_BLK, None), P(GRP_BLK, None), P(), P())
    return jax.shard_map(
        shards, mesh=split, in_specs=placed, out_specs=P(GRP_BLK, None), check_vma=False
    )
```

```python
import functools

import jax
import jax.numpy as jnp
from jax import lax
from jax.experimental import pallas as pl
from jax.experimental.pallas import tpu as pltpu
from jax.sharding import Mesh
from jax.sharding import PartitionSpec as P

SEQ = 64
ITERS = 4
ALL = ("side", "pair", "blk_0", "blk_1", "core")
OWNERS = ("pair", "blk_0", "blk_1")
TILE = 128
PIECES = 8

damping_rate = 0.5
power_steps = 3
STEP = 256


def mxu(a, b, dims):
    return lax.dot_general(a, b, (dims, ((), ())), preferred_element_type=jnp.float32)


def as_three(row):
    high = row.astype(jnp.bfloat16).astype(jnp.float32)
    rest = row - high
    mid = rest.astype(jnp.bfloat16).astype(jnp.float32)
    low = rest - mid
    turn = lax.broadcasted_iota(jnp.int32, (16, row.shape[1]), 0)
    rows = jnp.where(turn == 0, high, jnp.where(turn == 1, mid, jnp.where(turn == 2, low, 0.0)))
    return rows.astype(jnp.bfloat16)


def feature_kernel(
    act_ref, grad_ref, pa_ref, po_ref, out_ref, act_low, grad_low, feats, by_coord
):
    step = pl.program_id(0)
    steps = pl.num_programs(0)
    tokens = act_ref.shape[0]
    rows = pl.ds(pl.multiple_of(step * tokens, tokens), tokens)
    act_low[rows, :] = mxu(act_ref[...], pa_ref[...], ((1,), (0,))).astype(jnp.bfloat16)
    grad_low[rows, :] = mxu(grad_ref[...], po_ref[...], ((1,), (0,))).astype(jnp.bfloat16)
    blocks, examples, width = by_coord.shape
    per = width // grad_low.shape[1]
    cols = grad_low.shape[1]

    def eight(half):
        for e in range(8):
            at = pl.ds((half * 8 + e) * SEQ, SEQ)
            feats[e] = mxu(act_low[at, :], grad_low[at, :], ((0,), (0,)))
        turned = jnp.swapaxes(feats[...], 0, 1)
        turned = turned.reshape(blocks, per, 8, cols)
        for j in range(per):
            by_coord[:, half * 8 : half * 8 + 8, j * cols : (j + 1) * cols] = turned[:, j]

    @pl.when(step == steps // 2)
    def _():
        eight(0)

    @pl.when(step == steps - 1)
    def _():
        eight(1)
        acc = jnp.zeros((examples, width), jnp.float32)
        for k in range(blocks):
            low = by_coord[k].astype(jnp.bfloat16)
            out_ref[k, :, :width] = low
            wide = low.astype(jnp.float32)
            acc = acc + wide * wide
        part = jnp.zeros((8, TILE), jnp.float32)
        for r in range(0, examples, 8):
            for c in range(0, width, TILE):
                part = part + acc[r : r + 8, c : c + TILE]
        tail = as_three(jnp.sum(part, axis=0, keepdims=True))
        for k in range(blocks):
            out_ref[k, :, width:] = tail


def features_of(activations, out_grads, proj_act, proj_out, blocks):
    arguments = (activations, out_grads, proj_act, proj_out)
    tokens, depth = activations.shape
    examples = tokens // SEQ
    ra, rb = proj_act.shape[1], proj_out.shape[1]
    width = ra * rb // blocks
    steps = 4
    size = tokens // steps
    return pl.pallas_call(
        feature_kernel,
        grid=(steps,),
        in_specs=[
            pl.BlockSpec((size, depth), lambda i: (i, 0)),
            pl.BlockSpec((size, depth), lambda i: (i, 0)),
            pl.BlockSpec((depth, ra), lambda i: (0, 0), pipeline_mode=pl.Buffered(1)),
            pl.BlockSpec((depth, rb), lambda i: (0, 0), pipeline_mode=pl.Buffered(1)),
        ],
        out_specs=pl.BlockSpec((blocks, examples, width + TILE), lambda i: (0, 0, 0)),
        out_shape=jax.ShapeDtypeStruct((blocks, examples, width + TILE), jnp.bfloat16),
        scratch_shapes=[
            pltpu.VMEM((tokens, ra), jnp.bfloat16),
            pltpu.VMEM((tokens, rb), jnp.bfloat16),
            pltpu.VMEM((8, ra, rb), jnp.float32),
            pltpu.VMEM((blocks, examples, width), jnp.float32),
        ],
        compiler_params=pltpu.CompilerParams(
            dimension_semantics=("arbitrary",), vmem_limit_bytes=32 << 20
        ),
        name="features",
    )(*(pltpu.with_memory_space_constraint(x, pltpu.HBM) for x in arguments))


NEAR = ((0, 1), (0, 2), (0, 3), (1, 2), (1, 3))


def row_and_column(size=TILE):
    shape = (size, size)
    return lax.broadcasted_iota(jnp.int32, shape, 0), lax.broadcasted_iota(jnp.int32, shape, 1)


def tile_at(index, count=1):
    if isinstance(index, int):
        return slice(index * TILE, (index + count) * TILE)
    return pl.ds(pl.multiple_of(index * TILE, TILE), count * TILE)


def gram_kernel(core_ref, mine_ref, other_ref, own_ref, sum_ref, send_ref):
    core = core_ref[0]
    width = mine_ref.shape[1] - TILE
    squares = jnp.sum(
        mine_ref[:, width:].astype(jnp.float32) + other_ref[:, width:].astype(jnp.float32),
        axis=0,
        keepdims=True,
    )
    sum_ref[...] = jnp.broadcast_to(squares, sum_ref.shape)
    row, column = row_and_column()

    def product(left, right):
        dims = ((0,), (0,))
        return mxu(mine_ref[:, left], mine_ref[:, right], dims) + mxu(
            other_ref[:, left], other_ref[:, right], dims
        )

    diagonals = []
    for n in range(2):
        first = 4 * core + 2 * n
        left = tile_at(first, 2)
        near = product(left, left)
        after = product(left, tile_at(lax.rem(first + 2, 8), 2))
        far = product(tile_at(2 * n + core), tile_at(2 * n + 4, 2))
        packed = jnp.where(row <= column, near[:TILE, :TILE], near[TILE:, TILE:])
        inner = jnp.where(row == column, near[TILE:, TILE:], 0.0)
        diagonals.append(jnp.sum(inner, axis=0, keepdims=True))
        pieces = (
            packed,
            near[:TILE, TILE:],
            after[:TILE, :TILE],
            after[:TILE, TILE:],
            after[TILE:, :TILE],
            after[TILE:, TILE:],
            far[:, :TILE],
            far[:, TILE:],
        )
        for m, piece in enumerate(pieces):
            own_ref[tile_at(n * PIECES + m), :] = piece
            send_ref[tile_at(n * PIECES + m), :] = piece.astype(jnp.bfloat16)
    turn = lax.broadcasted_iota(jnp.int32, (16, TILE), 0)
    last = jnp.where(turn == 3, diagonals[0], jnp.where(turn == 4, diagonals[1], 0.0))
    rows = slice(2 * PIECES * TILE, 2 * PIECES * TILE + 16)
    own_ref[rows, :] = last
    send_ref[rows, :] = as_three(squares) + last.astype(jnp.bfloat16)


def gram_parts(core, mine, other):
    count = 2 * PIECES * TILE + 16
    vmem = pl.BlockSpec(memory_space=pltpu.VMEM)
    return pl.pallas_call(
        gram_kernel,
        in_specs=[pl.BlockSpec(memory_space=pltpu.SMEM), vmem, vmem],
        out_specs=[vmem, vmem, vmem],
        out_shape=[
            jax.ShapeDtypeStruct((count, TILE), jnp.float32),
            jax.ShapeDtypeStruct((8, TILE), jnp.float32),
            jax.ShapeDtypeStruct((count, TILE), jnp.bfloat16),
        ],
        compiler_params=pltpu.CompilerParams(vmem_limit_bytes=16 << 20),
        name="gram_parts",
    )(core, mine, other)


def put_pieces(half, ref, gram):
    row, column = row_and_column()
    last = ref[2 * PIECES * TILE :, :].astype(jnp.float32)
    for n in range(2):
        first = 4 * half + 2 * n
        packed = ref[tile_at(n * PIECES), :].astype(jnp.float32)
        turned = packed.T
        upper = jnp.where(row <= column, packed, turned)
        inner = jnp.where(row < column, turned, last[3 + n : 4 + n, :])
        lower = jnp.where(row > column, packed, inner)
        gram[tile_at(first), tile_at(first)] = upper.astype(jnp.bfloat16)
        gram[tile_at(first + 1), tile_at(first + 1)] = lower.astype(jnp.bfloat16)
        spots = [(lax.rem(first + i, 8), lax.rem(first + j, 8)) for i, j in NEAR]
        spots += [(2 * n + half, 2 * n + 4), (2 * n + half, 2 * n + 5)]
        for m, (i, j) in enumerate(spots):
            piece = ref[tile_at(n * PIECES + 1 + m), :]
            gram[tile_at(i), tile_at(j)] = piece
            gram[tile_at(j), tile_at(i)] = piece.T


def spread_kernel(core_ref, half_ref, gram_ref):
    put_pieces(core_ref[0], half_ref, gram_ref)


def spread(core, half, width):
    return pl.pallas_call(
        spread_kernel,
        in_specs=[pl.BlockSpec(memory_space=pltpu.SMEM), pl.BlockSpec(memory_space=pltpu.VMEM)],
        out_specs=pl.BlockSpec(memory_space=pltpu.VMEM),
        out_shape=jax.ShapeDtypeStruct((width, width), jnp.bfloat16),
        compiler_params=pltpu.CompilerParams(vmem_limit_bytes=16 << 20),
        name="spread",
    )(core, half)


def order_kernel(core_ref, mine_ref, other_ref, out_ref, ordered):
    core = core_ref[0]
    groups, width, examples = out_ref.shape
    piece = 16
    count = examples // (2 * piece)
    for g in range(groups):
        for p in range(count):
            at = slice((g * count + p) * piece, (g * count + p + 1) * piece)
            for which, ref in ((core, mine_ref), (1 - core, other_ref)):
                to = pl.multiple_of(p * 2 * piece + which * piece, piece)
                ordered[g, pl.ds(to, piece), :] = ref[at, :width]
        out_ref[g] = ordered[g].T


def in_order(core, mine, other, width):
    vmem = pl.BlockSpec(memory_space=pltpu.VMEM)
    examples = mine.shape[0]
    return pl.pallas_call(
        order_kernel,
        in_specs=[pl.BlockSpec(memory_space=pltpu.SMEM), vmem, vmem],
        out_specs=vmem,
        out_shape=jax.ShapeDtypeStruct((2, width, examples), jnp.bfloat16),
        scratch_shapes=[pltpu.VMEM((2, examples, width), jnp.bfloat16)],
        compiler_params=pltpu.CompilerParams(vmem_limit_bytes=16 << 20),
        name="in_order",
    )(core, mine, other)


def solve_kernel(
    coords,
    core_ref,
    sum_ref,
    far_sum_ref,
    rest_ref,
    started_ref,
    mine_ref,
    group_ref,
    out_ref,
    gram,
    first,
    second,
    low,
):
    put_pieces(1 - core_ref[0], rest_ref, gram)
    width = gram.shape[0]
    examples = mine_ref.shape[0]
    columns = [slice(c, c + STEP) for c in range(0, width, STEP)]

    def operate(field):
        for at in columns:
            yield at, mxu(field(), gram[:, at], ((1,), (0,)))

    vector = jnp.full((1, width), 1.0 / width**0.5, jnp.float32)
    for _ in range(power_steps):
        image = mxu(as_three(vector), gram[...], ((1,), (0,)))
        image = jnp.sum(image, axis=0, keepdims=True)
        radius = jnp.sqrt(jnp.sum(image * image, axis=1, keepdims=True) + 1e-06)
        vector = image / radius
    total = jnp.sum(sum_ref[0:1, :], axis=1, keepdims=True) + jnp.sum(
        jnp.sum(far_sum_ref[...].astype(jnp.float32)[0:3, :], axis=0, keepdims=True), axis=1, keepdims=True
    )
    damping = damping_rate * (total / coords)
    center = damping + radius
    strides = [1.0 / center]
    momenta = []
    for sweep in range(1, ITERS):
        if sweep == 1:
            momenta.append(0.5 * (radius * strides[-1]) ** 2)
        else:
            momenta.append((0.5 * radius * strides[-1]) ** 2)
        strides.append(1.0 / (center - momenta[-1] / strides[-1]))
    keep = [1.0 + m - s * damping for m, s in zip(momenta, strides)]
    weights = (
        strides[1] - strides[3] * momenta[1],
        strides[2] + strides[3] * keep[2],
        strides[3] * strides[2],
    )

    def right_side(at):
        return mine_ref[:, at].astype(jnp.float32)

    for at, value in operate(lambda: mine_ref[:, :width]):
        value = keep[0] * right_side(at) - strides[0] * value
        first[:, at] = value
        low[0, :, at] = value.astype(jnp.bfloat16)
    for at, value in operate(lambda: low[0]):
        value = keep[1] * first[:, at] - momenta[0] * right_side(at) - strides[1] * value
        second[:, at] = value
        low[1, :, at] = value.astype(jnp.bfloat16)
    for at, value in operate(lambda: low[1]):
        value = (
            strides[0] * right_side(at)
            + weights[0] * first[:, at]
            + weights[1] * second[:, at]
            - weights[2] * value
        )
        low[0, :, at] = value.astype(jnp.bfloat16)
    half = examples // 2
    for g in range(2):
        out_ref[g * half : (g + 1) * half, :] = mxu(
            low[0, g * half : (g + 1) * half, :],
            group_ref[g],
            ((1,), (0,)),
        ).astype(out_ref.dtype)


def block_scores(coords, core, squares, far_squares, rest, started, mine, rows):
    vmem = pl.BlockSpec(memory_space=pltpu.VMEM)
    smem = pl.BlockSpec(memory_space=pltpu.SMEM)
    examples = mine.shape[0]
    width = started.shape[0]
    field = (examples, width)
    return pl.pallas_call(
        functools.partial(solve_kernel, coords),
        in_specs=[smem] + [vmem] * 6,
        out_specs=[vmem, vmem],
        out_shape=[
            jax.ShapeDtypeStruct((examples, examples), jnp.bfloat16),
            jax.ShapeDtypeStruct((width, width), jnp.bfloat16),
        ],
        scratch_shapes=[
            pltpu.VMEM(field, jnp.float32),
            pltpu.VMEM(field, jnp.float32),
            pltpu.VMEM((2,) + field, jnp.bfloat16),
        ],
        input_output_aliases={4: 1},
        compiler_params=pltpu.CompilerParams(vmem_limit_bytes=32 << 20),
        name="solve",
    )(core, squares, far_squares, rest, started, mine, rows)[0]


def shifted(value, axis, shift):
    size = lax.axis_size(axis)
    return lax.ppermute(value, axis, [(i, (i + shift) % size) for i in range(size)])


def shards(activations, out_grads, proj_act, proj_out):
    examples = activations.shape[0] // SEQ
    coords = proj_act.shape[1] * proj_out.shape[1]
    blocks = lax.axis_size(OWNERS)
    by_block = features_of(activations, out_grads, proj_act, proj_out, blocks)
    arrived = lax.all_to_all(by_block, OWNERS, 0, 0, tiled=True)
    mine = arrived.reshape(blocks * examples, -1)
    other = shifted(mine, "core", 1)

    core = lax.axis_index("core").astype(jnp.int32).reshape(1)
    own, squares, send = gram_parts(core, mine, other)
    across = shifted(send, "side", 1)
    count = own.shape[0]
    width = coords // blocks
    mine_later, other_later, _ = lax.optimization_barrier((mine, other, send))
    rows = in_order(core, mine_later, other_later, width)
    half = (own + across.astype(jnp.float32)).astype(jnp.bfloat16)
    rest = shifted(half, "core", 1)
    started = spread(core, half, width)
    term = block_scores(coords, core, squares, across[count - 16 :], rest, started, mine, rows)
    terms = lax.all_to_all(term.reshape(blocks, examples, -1), OWNERS, 0, 0, tiled=True)
    scores = jnp.sum(terms.astype(jnp.float32), axis=0)
    return scores * float(examples * lax.axis_size(("side", "pair")))


def solution(mesh):
    split = Mesh(mesh.devices.reshape(2, 2, 4, 4, 2), ALL)
    placed = (P(ALL, None), P(ALL, None), P(), P())
    return jax.shard_map(shards, mesh=split, in_specs=placed, out_specs=P(ALL, None), check_vma=False)
```

```python
import functools

import jax
import jax.numpy as jnp
from jax import lax
from jax.experimental import pallas as pl
from jax.experimental.pallas import tpu as pltpu
from jax.sharding import Mesh
from jax.sharding import PartitionSpec as P

SEQ = 64
ITERS = 4
ALL = ("side", "pair", "blk_0", "blk_1", "core")
OWNERS = ("pair", "blk_0", "blk_1")
TILE = 128
PIECES = 8

damping_rate = 0.5
power_steps = 3
STEP = 256


def mxu(a, b, dims):
    return lax.dot_general(a, b, (dims, ((), ())), preferred_element_type=jnp.float32)


def as_three(row):
    high = row.astype(jnp.bfloat16).astype(jnp.float32)
    rest = row - high
    mid = rest.astype(jnp.bfloat16).astype(jnp.float32)
    low = rest - mid
    turn = lax.broadcasted_iota(jnp.int32, (16, row.shape[1]), 0)
    rows = jnp.where(turn == 0, high, jnp.where(turn == 1, mid, jnp.where(turn == 2, low, 0.0)))
    return rows.astype(jnp.bfloat16)


def feature_kernel(
    side_ref, act_ref, grad_ref, pa_ref, po_ref, out_ref, act_low, grad_low, feats, by_coord
):
    step = pl.program_id(0)
    steps = pl.num_programs(0)
    tokens = act_ref.shape[0]
    rows = pl.ds(pl.multiple_of(step * tokens, tokens), tokens)
    act_low[rows, :] = mxu(act_ref[...], pa_ref[...], ((1,), (0,))).astype(jnp.bfloat16)
    grad_low[rows, :] = mxu(grad_ref[...], po_ref[...], ((1,), (0,))).astype(jnp.bfloat16)
    blocks, examples, width = by_coord.shape
    per = width // grad_low.shape[1]
    cols = grad_low.shape[1]

    def eight(half):
        for e in range(8):
            at = pl.ds((half * 8 + e) * SEQ, SEQ)
            feats[e] = mxu(act_low[at, :], grad_low[at, :], ((0,), (0,)))
        turned = jnp.swapaxes(feats[...], 0, 1)
        turned = turned.reshape(blocks, per, 8, cols)
        for j in range(per):
            by_coord[:, half * 8 : half * 8 + 8, j * cols : (j + 1) * cols] = turned[:, j]

    @pl.when(step == steps // 2)
    def _():
        eight(0)

    @pl.when(step == steps - 1)
    def _():
        eight(1)
        acc = jnp.zeros((examples, width), jnp.float32)
        turn = side_ref[0] * (blocks // 2)
        for k in range(blocks):
            low = by_coord[k].astype(jnp.bfloat16)
            out_ref[lax.rem(k + turn, blocks), :, :width] = low
            wide = low.astype(jnp.float32)
            acc = acc + wide * wide
        part = jnp.zeros((8, TILE), jnp.float32)
        for r in range(0, examples, 8):
            for c in range(0, width, TILE):
                part = part + acc[r : r + 8, c : c + TILE]
        tail = as_three(jnp.sum(part, axis=0, keepdims=True))
        for k in range(blocks):
            out_ref[k, :, width:] = tail


def features_of(side, activations, out_grads, proj_act, proj_out, blocks):
    arguments = (activations, out_grads, proj_act, proj_out)
    tokens, depth = activations.shape
    examples = tokens // SEQ
    ra, rb = proj_act.shape[1], proj_out.shape[1]
    width = ra * rb // blocks
    steps = 4
    size = tokens // steps
    return pl.pallas_call(
        feature_kernel,
        grid=(steps,),
        in_specs=[
            pl.BlockSpec(memory_space=pltpu.SMEM),
            pl.BlockSpec((size, depth), lambda i: (i, 0)),
            pl.BlockSpec((size, depth), lambda i: (i, 0)),
            pl.BlockSpec((depth, ra), lambda i: (0, 0), pipeline_mode=pl.Buffered(1)),
            pl.BlockSpec((depth, rb), lambda i: (0, 0), pipeline_mode=pl.Buffered(1)),
        ],
        out_specs=pl.BlockSpec((blocks, examples, width + TILE), lambda i: (0, 0, 0)),
        out_shape=jax.ShapeDtypeStruct((blocks, examples, width + TILE), jnp.bfloat16),
        scratch_shapes=[
            pltpu.VMEM((tokens, ra), jnp.bfloat16),
            pltpu.VMEM((tokens, rb), jnp.bfloat16),
            pltpu.VMEM((8, ra, rb), jnp.float32),
            pltpu.VMEM((blocks, examples, width), jnp.float32),
        ],
        compiler_params=pltpu.CompilerParams(
            dimension_semantics=("arbitrary",), vmem_limit_bytes=32 << 20
        ),
        name="features",
    )(side, *(pltpu.with_memory_space_constraint(x, pltpu.HBM) for x in arguments))


NEAR = ((0, 1), (0, 2), (0, 3), (1, 2), (1, 3))


def row_and_column(size=TILE):
    shape = (size, size)
    return lax.broadcasted_iota(jnp.int32, shape, 0), lax.broadcasted_iota(jnp.int32, shape, 1)


def tile_at(index, count=1):
    if isinstance(index, int):
        return slice(index * TILE, (index + count) * TILE)
    return pl.ds(pl.multiple_of(index * TILE, TILE), count * TILE)


def gram_kernel(core_ref, mine_ref, other_ref, own_ref, sum_ref, send_ref):
    core = core_ref[0]
    width = mine_ref.shape[1] - TILE
    squares = jnp.sum(
        mine_ref[:, width:].astype(jnp.float32) + other_ref[:, width:].astype(jnp.float32),
        axis=0,
        keepdims=True,
    )
    sum_ref[...] = jnp.broadcast_to(squares, sum_ref.shape)
    row, column = row_and_column()

    def product(left, right):
        dims = ((0,), (0,))
        return mxu(mine_ref[:, left], mine_ref[:, right], dims) + mxu(
            other_ref[:, left], other_ref[:, right], dims
        )

    diagonals = []
    for n in range(2):
        first = 4 * core + 2 * n
        left = tile_at(first, 2)
        near = product(left, left)
        after = product(left, tile_at(lax.rem(first + 2, 8), 2))
        far = product(tile_at(2 * n + core), tile_at(2 * n + 4, 2))
        packed = jnp.where(row <= column, near[:TILE, :TILE], near[TILE:, TILE:])
        inner = jnp.where(row == column, near[TILE:, TILE:], 0.0)
        diagonals.append(jnp.sum(inner, axis=0, keepdims=True))
        pieces = (
            packed,
            near[:TILE, TILE:],
            after[:TILE, :TILE],
            after[:TILE, TILE:],
            after[TILE:, :TILE],
            after[TILE:, TILE:],
            far[:, :TILE],
            far[:, TILE:],
        )
        for m, piece in enumerate(pieces):
            own_ref[tile_at(n * PIECES + m), :] = piece
            send_ref[tile_at(n * PIECES + m), :] = piece.astype(jnp.bfloat16)
    turn = lax.broadcasted_iota(jnp.int32, (16, TILE), 0)
    last = jnp.where(turn == 3, diagonals[0], jnp.where(turn == 4, diagonals[1], 0.0))
    rows = slice(2 * PIECES * TILE, 2 * PIECES * TILE + 16)
    own_ref[rows, :] = last
    send_ref[rows, :] = as_three(squares) + last.astype(jnp.bfloat16)


def gram_parts(core, mine, other):
    count = 2 * PIECES * TILE + 16
    vmem = pl.BlockSpec(memory_space=pltpu.VMEM)
    return pl.pallas_call(
        gram_kernel,
        in_specs=[pl.BlockSpec(memory_space=pltpu.SMEM), vmem, vmem],
        out_specs=[vmem, vmem, vmem],
        out_shape=[
            jax.ShapeDtypeStruct((count, TILE), jnp.float32),
            jax.ShapeDtypeStruct((8, TILE), jnp.float32),
            jax.ShapeDtypeStruct((count, TILE), jnp.bfloat16),
        ],
        compiler_params=pltpu.CompilerParams(vmem_limit_bytes=16 << 20),
        name="gram_parts",
    )(core, mine, other)


def put_pieces(half, ref, gram):
    row, column = row_and_column()
    last = ref[2 * PIECES * TILE :, :].astype(jnp.float32)
    for n in range(2):
        first = 4 * half + 2 * n
        packed = ref[tile_at(n * PIECES), :].astype(jnp.float32)
        turned = packed.T
        upper = jnp.where(row <= column, packed, turned)
        inner = jnp.where(row < column, turned, last[3 + n : 4 + n, :])
        lower = jnp.where(row > column, packed, inner)
        gram[tile_at(first), tile_at(first)] = upper.astype(jnp.bfloat16)
        gram[tile_at(first + 1), tile_at(first + 1)] = lower.astype(jnp.bfloat16)
        spots = [(lax.rem(first + i, 8), lax.rem(first + j, 8)) for i, j in NEAR]
        spots += [(2 * n + half, 2 * n + 4), (2 * n + half, 2 * n + 5)]
        for m, (i, j) in enumerate(spots):
            piece = ref[tile_at(n * PIECES + 1 + m), :]
            gram[tile_at(i), tile_at(j)] = piece
            gram[tile_at(j), tile_at(i)] = piece.T


def spread_kernel(core_ref, half_ref, gram_ref):
    put_pieces(core_ref[0], half_ref, gram_ref)


def spread(core, half, width):
    return pl.pallas_call(
        spread_kernel,
        in_specs=[pl.BlockSpec(memory_space=pltpu.SMEM), pl.BlockSpec(memory_space=pltpu.VMEM)],
        out_specs=pl.BlockSpec(memory_space=pltpu.VMEM),
        out_shape=jax.ShapeDtypeStruct((width, width), jnp.bfloat16),
        compiler_params=pltpu.CompilerParams(vmem_limit_bytes=16 << 20),
        name="spread",
    )(core, half)


def order_kernel(core_ref, mine_ref, other_ref, out_ref, ordered):
    core = core_ref[0]
    groups, width, examples = out_ref.shape
    piece = 16
    count = examples // (2 * piece)
    for g in range(groups):
        for p in range(count):
            at = slice((g * count + p) * piece, (g * count + p + 1) * piece)
            for which, ref in ((core, mine_ref), (1 - core, other_ref)):
                to = pl.multiple_of(p * 2 * piece + which * piece, piece)
                ordered[g, pl.ds(to, piece), :] = ref[at, :width]
        out_ref[g] = ordered[g].T


def in_order(core, mine, other, width):
    vmem = pl.BlockSpec(memory_space=pltpu.VMEM)
    examples = mine.shape[0]
    return pl.pallas_call(
        order_kernel,
        in_specs=[pl.BlockSpec(memory_space=pltpu.SMEM), vmem, vmem],
        out_specs=vmem,
        out_shape=jax.ShapeDtypeStruct((2, width, examples), jnp.bfloat16),
        scratch_shapes=[pltpu.VMEM((2, examples, width), jnp.bfloat16)],
        compiler_params=pltpu.CompilerParams(vmem_limit_bytes=16 << 20),
        name="in_order",
    )(core, mine, other)


def solve_kernel(
    coords,
    core_ref,
    sum_ref,
    far_sum_ref,
    rest_ref,
    started_ref,
    mine_ref,
    group_ref,
    out_ref,
    gram,
    first,
    second,
    low,
):
    put_pieces(1 - core_ref[0], rest_ref, gram)
    width = gram.shape[0]
    examples = mine_ref.shape[0]
    columns = [slice(c, c + STEP) for c in range(0, width, STEP)]

    def operate(field):
        for at in columns:
            yield at, mxu(field(), gram[:, at], ((1,), (0,)))

    vector = jnp.full((1, width), 1.0 / width**0.5, jnp.float32)
    for _ in range(power_steps):
        image = mxu(as_three(vector), gram[...], ((1,), (0,)))
        image = jnp.sum(image, axis=0, keepdims=True)
        radius = jnp.sqrt(jnp.sum(image * image, axis=1, keepdims=True) + 1e-06)
        vector = image / radius
    total = jnp.sum(sum_ref[0:1, :], axis=1, keepdims=True) + jnp.sum(
        jnp.sum(far_sum_ref[...].astype(jnp.float32)[0:3, :], axis=0, keepdims=True), axis=1, keepdims=True
    )
    damping = damping_rate * (total / coords)
    center = damping + radius
    strides = [1.0 / center]
    momenta = []
    for sweep in range(1, ITERS):
        if sweep == 1:
            momenta.append(0.5 * (radius * strides[-1]) ** 2)
        else:
            momenta.append((0.5 * radius * strides[-1]) ** 2)
        strides.append(1.0 / (center - momenta[-1] / strides[-1]))
    keep = [1.0 + m - s * damping for m, s in zip(momenta, strides)]
    weights = (
        strides[1] - strides[3] * momenta[1],
        strides[2] + strides[3] * keep[2],
        strides[3] * strides[2],
    )

    def right_side(at):
        return mine_ref[:, at].astype(jnp.float32)

    for at, value in operate(lambda: mine_ref[:, :width]):
        value = keep[0] * right_side(at) - strides[0] * value
        first[:, at] = value
        low[0, :, at] = value.astype(jnp.bfloat16)
    for at, value in operate(lambda: low[0]):
        value = keep[1] * first[:, at] - momenta[0] * right_side(at) - strides[1] * value
        second[:, at] = value
        low[1, :, at] = value.astype(jnp.bfloat16)
    for at, value in operate(lambda: low[1]):
        value = (
            strides[0] * right_side(at)
            + weights[0] * first[:, at]
            + weights[1] * second[:, at]
            - weights[2] * value
        )
        low[0, :, at] = value.astype(jnp.bfloat16)
    half = examples // 2
    for g in range(2):
        out_ref[g * half : (g + 1) * half, :] = mxu(
            low[0, g * half : (g + 1) * half, :],
            group_ref[g],
            ((1,), (0,)),
        ).astype(out_ref.dtype)


def block_scores(coords, core, squares, far_squares, rest, started, mine, rows):
    vmem = pl.BlockSpec(memory_space=pltpu.VMEM)
    smem = pl.BlockSpec(memory_space=pltpu.SMEM)
    examples = mine.shape[0]
    width = started.shape[0]
    field = (examples, width)
    return pl.pallas_call(
        functools.partial(solve_kernel, coords),
        in_specs=[smem] + [vmem] * 6,
        out_specs=[vmem, vmem],
        out_shape=[
            jax.ShapeDtypeStruct((examples, examples), jnp.bfloat16),
            jax.ShapeDtypeStruct((width, width), jnp.bfloat16),
        ],
        scratch_shapes=[
            pltpu.VMEM(field, jnp.float32),
            pltpu.VMEM(field, jnp.float32),
            pltpu.VMEM((2,) + field, jnp.bfloat16),
        ],
        input_output_aliases={4: 1},
        compiler_params=pltpu.CompilerParams(vmem_limit_bytes=32 << 20),
        name="solve",
    )(core, squares, far_squares, rest, started, mine, rows)[0]


def shifted(value, axis, shift):
    size = lax.axis_size(axis)
    return lax.ppermute(value, axis, [(i, (i + shift) % size) for i in range(size)])


def shards(activations, out_grads, proj_act, proj_out):
    examples = activations.shape[0] // SEQ
    coords = proj_act.shape[1] * proj_out.shape[1]
    blocks = lax.axis_size(OWNERS)
    side = lax.axis_index("side").astype(jnp.int32).reshape(1)
    by_block = features_of(side, activations, out_grads, proj_act, proj_out, blocks)
    arrived = lax.all_to_all(by_block, OWNERS, 0, 0, tiled=True)
    mine = arrived.reshape(blocks * examples, -1)
    other = shifted(mine, "core", 1)

    core = lax.axis_index("core").astype(jnp.int32).reshape(1)
    own, squares, send = gram_parts(core, mine, other)
    across = lax.ppermute(send, ("side", "pair"), [(0, 3), (3, 0), (1, 2), (2, 1)])
    count = own.shape[0]
    width = coords // blocks
    mine_later, other_later, _ = lax.optimization_barrier((mine, other, send))
    rows = in_order(core, mine_later, other_later, width)
    half = (own + across.astype(jnp.float32)).astype(jnp.bfloat16)
    rest = shifted(half, "core", 1)
    started = spread(core, half, width)
    term = block_scores(coords, core, squares, across[count - 16 :], rest, started, mine, rows)
    terms = lax.all_to_all(term.reshape(blocks, examples, -1), OWNERS, 0, 0, tiled=True)
    scores = jnp.sum(terms.astype(jnp.float32), axis=0)
    return scores * float(examples * lax.axis_size(("side", "pair")))


def solution(mesh):
    split = Mesh(mesh.devices.reshape(2, 2, 4, 4, 2), ALL)
    placed = (P(ALL, None), P(ALL, None), P(), P())
    return jax.shard_map(shards, mesh=split, in_specs=placed, out_specs=P(ALL, None), check_vma=False)
```

```python
import functools

import jax
import jax.numpy as jnp
from jax import lax
from jax.experimental import pallas as pl
from jax.experimental.pallas import tpu as pltpu
from jax.sharding import Mesh
from jax.sharding import PartitionSpec as P

SEQ = 64
ITERS = 4
ALL = ("side", "pair", "blk_0", "blk_1", "core")
OWNERS = ("pair", "blk_0", "blk_1")
TILE = 128
PIECES = 8

damping_rate = 0.5
power_steps = 3
STEP = 256


def mxu(a, b, dims):
    return lax.dot_general(a, b, (dims, ((), ())), preferred_element_type=jnp.float32)


def as_three(row):
    high = row.astype(jnp.bfloat16).astype(jnp.float32)
    rest = row - high
    mid = rest.astype(jnp.bfloat16).astype(jnp.float32)
    low = rest - mid
    turn = lax.broadcasted_iota(jnp.int32, (16, row.shape[1]), 0)
    rows = jnp.where(turn == 0, high, jnp.where(turn == 1, mid, jnp.where(turn == 2, low, 0.0)))
    return rows.astype(jnp.bfloat16)


def feature_kernel(
    side_ref, act_ref, grad_ref, pa_ref, po_ref, out_ref, act_low, grad_low, feats, by_coord
):
    step = pl.program_id(0)
    steps = pl.num_programs(0)
    tokens = act_ref.shape[0]
    rows = pl.ds(pl.multiple_of(step * tokens, tokens), tokens)
    act_low[rows, :] = mxu(act_ref[...], pa_ref[...], ((1,), (0,))).astype(jnp.bfloat16)
    grad_low[rows, :] = mxu(grad_ref[...], po_ref[...], ((1,), (0,))).astype(jnp.bfloat16)
    blocks, examples, width = by_coord.shape
    per = width // grad_low.shape[1]
    cols = grad_low.shape[1]

    def eight(half):
        for e in range(8):
            at = pl.ds((half * 8 + e) * SEQ, SEQ)
            feats[e] = mxu(act_low[at, :], grad_low[at, :], ((0,), (0,)))
        turned = jnp.swapaxes(feats[...], 0, 1)
        turned = turned.reshape(blocks, per, 8, cols)
        for j in range(per):
            by_coord[:, half * 8 : half * 8 + 8, j * cols : (j + 1) * cols] = turned[:, j]

    @pl.when(step == steps // 2)
    def _():
        eight(0)

    @pl.when(step == steps - 1)
    def _():
        eight(1)
        acc = jnp.zeros((examples, width), jnp.float32)
        turn = side_ref[0] * (blocks // 2)
        for k in range(blocks):
            low = by_coord[k].astype(jnp.bfloat16)
            out_ref[lax.rem(k + turn, blocks), :, :width] = low
            wide = low.astype(jnp.float32)
            acc = acc + wide * wide
        part = jnp.zeros((8, TILE), jnp.float32)
        for r in range(0, examples, 8):
            for c in range(0, width, TILE):
                part = part + acc[r : r + 8, c : c + TILE]
        tail = as_three(jnp.sum(part, axis=0, keepdims=True))
        for k in range(blocks):
            out_ref[k, :, width:] = tail


def features_of(side, activations, out_grads, proj_act, proj_out, blocks):
    arguments = (activations, out_grads, proj_act, proj_out)
    tokens, depth = activations.shape
    examples = tokens // SEQ
    ra, rb = proj_act.shape[1], proj_out.shape[1]
    width = ra * rb // blocks
    steps = 2
    size = tokens // steps
    return pl.pallas_call(
        feature_kernel,
        grid=(steps,),
        in_specs=[
            pl.BlockSpec(memory_space=pltpu.SMEM),
            pl.BlockSpec((size, depth), lambda i: (i, 0)),
            pl.BlockSpec((size, depth), lambda i: (i, 0)),
            pl.BlockSpec((depth, ra), lambda i: (0, 0), pipeline_mode=pl.Buffered(1)),
            pl.BlockSpec((depth, rb), lambda i: (0, 0), pipeline_mode=pl.Buffered(1)),
        ],
        out_specs=pl.BlockSpec((blocks, examples, width + TILE), lambda i: (0, 0, 0)),
        out_shape=jax.ShapeDtypeStruct((blocks, examples, width + TILE), jnp.bfloat16),
        scratch_shapes=[
            pltpu.VMEM((tokens, ra), jnp.bfloat16),
            pltpu.VMEM((tokens, rb), jnp.bfloat16),
            pltpu.VMEM((8, ra, rb), jnp.float32),
            pltpu.VMEM((blocks, examples, width), jnp.float32),
        ],
        compiler_params=pltpu.CompilerParams(
            dimension_semantics=("arbitrary",), vmem_limit_bytes=32 << 20
        ),
        name="features",
    )(side, *(pltpu.with_memory_space_constraint(x, pltpu.HBM) for x in arguments))


NEAR = ((0, 1), (0, 2), (0, 3), (1, 2), (1, 3))


def row_and_column(size=TILE):
    shape = (size, size)
    return lax.broadcasted_iota(jnp.int32, shape, 0), lax.broadcasted_iota(jnp.int32, shape, 1)


def tile_at(index, count=1):
    if isinstance(index, int):
        return slice(index * TILE, (index + count) * TILE)
    return pl.ds(pl.multiple_of(index * TILE, TILE), count * TILE)


def gram_products(core, rows_ref):
    def product(left, right):
        return mxu(rows_ref[:, left], rows_ref[:, right], ((0,), (0,)))

    for n in range(2):
        first = 4 * core + 2 * n
        left = tile_at(first, 2)
        yield n, 0, product(left, left)
        yield n, 1, product(left, tile_at(lax.rem(first + 2, 8), 2))
        yield n, 2, product(tile_at(2 * n + core), tile_at(2 * n + 4, 2))


def part_of(n, m):
    first = (5 * n + 2 * m) * TILE
    return slice(first, first + (TILE if m == 2 else 2 * TILE))


def own_gram_kernel(core_ref, mine_ref, acc_ref):
    for n, m, value in gram_products(core_ref[0], mine_ref):
        acc_ref[part_of(n, m), :] = value


def gram_kernel(core_ref, acc_ref, mine_sum_ref, other_ref, own_ref, sum_ref, send_ref):
    width = other_ref.shape[1] - TILE
    squares = jnp.sum(
        mine_sum_ref[...].astype(jnp.float32) + other_ref[:, width:].astype(jnp.float32),
        axis=0,
        keepdims=True,
    )
    sum_ref[...] = jnp.broadcast_to(squares, sum_ref.shape)
    row, column = row_and_column()
    parts = {}
    for n, m, value in gram_products(core_ref[0], other_ref):
        parts[n, m] = acc_ref[part_of(n, m), :] + value
    diagonals = []
    for n in range(2):
        near, after, far = parts[n, 0], parts[n, 1], parts[n, 2]
        packed = jnp.where(row <= column, near[:TILE, :TILE], near[TILE:, TILE:])
        inner = jnp.where(row == column, near[TILE:, TILE:], 0.0)
        diagonals.append(jnp.sum(inner, axis=0, keepdims=True))
        pieces = (
            packed,
            near[:TILE, TILE:],
            after[:TILE, :TILE],
            after[:TILE, TILE:],
            after[TILE:, :TILE],
            after[TILE:, TILE:],
            far[:, :TILE],
            far[:, TILE:],
        )
        for m, piece in enumerate(pieces):
            own_ref[tile_at(n * PIECES + m), :] = piece
            send_ref[tile_at(n * PIECES + m), :] = piece.astype(jnp.bfloat16)
    turn = lax.broadcasted_iota(jnp.int32, (16, TILE), 0)
    last = jnp.where(turn == 3, diagonals[0], jnp.where(turn == 4, diagonals[1], 0.0))
    rows = slice(2 * PIECES * TILE, 2 * PIECES * TILE + 16)
    own_ref[rows, :] = last
    send_ref[rows, :] = as_three(squares) + last.astype(jnp.bfloat16)


def gram_parts(core, mine, other):
    count = 2 * PIECES * TILE + 16
    vmem = pl.BlockSpec(memory_space=pltpu.VMEM)
    smem = pl.BlockSpec(memory_space=pltpu.SMEM)
    params = pltpu.CompilerParams(vmem_limit_bytes=16 << 20)
    acc = pl.pallas_call(
        own_gram_kernel,
        in_specs=[smem, vmem],
        out_specs=vmem,
        out_shape=jax.ShapeDtypeStruct((10 * TILE, 2 * TILE), jnp.float32),
        compiler_params=params,
        name="own_gram",
    )(core, mine)
    return pl.pallas_call(
        gram_kernel,
        in_specs=[smem, vmem, vmem, vmem],
        out_specs=[vmem, vmem, vmem],
        out_shape=[
            jax.ShapeDtypeStruct((count, TILE), jnp.float32),
            jax.ShapeDtypeStruct((8, TILE), jnp.float32),
            jax.ShapeDtypeStruct((count, TILE), jnp.bfloat16),
        ],
        compiler_params=params,
        name="gram_parts",
    )(core, acc, mine[:, mine.shape[1] - TILE :], other)


def put_pieces(half, ref, gram):
    row, column = row_and_column()
    last = ref[2 * PIECES * TILE :, :].astype(jnp.float32)
    for n in range(2):
        first = 4 * half + 2 * n
        packed = ref[tile_at(n * PIECES), :].astype(jnp.float32)
        turned = packed.T
        upper = jnp.where(row <= column, packed, turned)
        inner = jnp.where(row < column, turned, last[3 + n : 4 + n, :])
        lower = jnp.where(row > column, packed, inner)
        gram[tile_at(first), tile_at(first)] = upper.astype(jnp.bfloat16)
        gram[tile_at(first + 1), tile_at(first + 1)] = lower.astype(jnp.bfloat16)
        spots = [(lax.rem(first + i, 8), lax.rem(first + j, 8)) for i, j in NEAR]
        spots += [(2 * n + half, 2 * n + 4), (2 * n + half, 2 * n + 5)]
        for m, (i, j) in enumerate(spots):
            piece = ref[tile_at(n * PIECES + 1 + m), :]
            gram[tile_at(i), tile_at(j)] = piece
            gram[tile_at(j), tile_at(i)] = piece.T


def spread_kernel(core_ref, half_ref, gram_ref):
    put_pieces(core_ref[0], half_ref, gram_ref)


def spread(core, half, width):
    return pl.pallas_call(
        spread_kernel,
        in_specs=[pl.BlockSpec(memory_space=pltpu.SMEM), pl.BlockSpec(memory_space=pltpu.VMEM)],
        out_specs=pl.BlockSpec(memory_space=pltpu.VMEM),
        out_shape=jax.ShapeDtypeStruct((width, width), jnp.bfloat16),
        compiler_params=pltpu.CompilerParams(vmem_limit_bytes=16 << 20),
        name="spread",
    )(core, half)


def order_kernel(core_ref, mine_ref, other_ref, out_ref, ordered):
    core = core_ref[0]
    groups, width, examples = out_ref.shape
    piece = 16
    count = examples // (2 * piece)
    for g in range(groups):
        for p in range(count):
            at = slice((g * count + p) * piece, (g * count + p + 1) * piece)
            for which, ref in ((core, mine_ref), (1 - core, other_ref)):
                to = pl.multiple_of(p * 2 * piece + which * piece, piece)
                ordered[g, pl.ds(to, piece), :] = ref[at, :width]
        out_ref[g] = ordered[g].T


def in_order(core, mine, other, width):
    vmem = pl.BlockSpec(memory_space=pltpu.VMEM)
    examples = mine.shape[0]
    return pl.pallas_call(
        order_kernel,
        in_specs=[pl.BlockSpec(memory_space=pltpu.SMEM), vmem, vmem],
        out_specs=vmem,
        out_shape=jax.ShapeDtypeStruct((2, width, examples), jnp.bfloat16),
        scratch_shapes=[pltpu.VMEM((2, examples, width), jnp.bfloat16)],
        compiler_params=pltpu.CompilerParams(vmem_limit_bytes=16 << 20),
        name="in_order",
    )(core, mine, other)


def solve_kernel(
    coords,
    core_ref,
    sum_ref,
    far_sum_ref,
    rest_ref,
    started_ref,
    mine_ref,
    group_ref,
    out_ref,
    gram,
    first,
    second,
    low,
):
    put_pieces(1 - core_ref[0], rest_ref, gram)
    width = gram.shape[0]
    examples = mine_ref.shape[0]
    columns = [slice(c, c + STEP) for c in range(0, width, STEP)]

    def operate(field):
        for at in columns:
            yield at, mxu(field(), gram[:, at], ((1,), (0,)))

    vector = jnp.full((1, width), 1.0 / width**0.5, jnp.float32)
    for _ in range(power_steps):
        image = mxu(as_three(vector), gram[...], ((1,), (0,)))
        image = jnp.sum(image, axis=0, keepdims=True)
        radius = jnp.sqrt(jnp.sum(image * image, axis=1, keepdims=True) + 1e-06)
        vector = image / radius
    total = jnp.sum(sum_ref[0:1, :], axis=1, keepdims=True) + jnp.sum(
        jnp.sum(far_sum_ref[...].astype(jnp.float32)[0:3, :], axis=0, keepdims=True),
        axis=1,
        keepdims=True,
    )
    damping = damping_rate * (total / coords)
    center = damping + radius
    strides = [1.0 / center]
    momenta = []
    for sweep in range(1, ITERS):
        if sweep == 1:
            momenta.append(0.5 * (radius * strides[-1]) ** 2)
        else:
            momenta.append((0.5 * radius * strides[-1]) ** 2)
        strides.append(1.0 / (center - momenta[-1] / strides[-1]))
    keep = [1.0 + m - s * damping for m, s in zip(momenta, strides)]
    weights = (
        strides[1] - strides[3] * momenta[1],
        strides[2] + strides[3] * keep[2],
        strides[3] * strides[2],
    )

    def right_side(at):
        return mine_ref[:, at].astype(jnp.float32)

    for at, value in operate(lambda: mine_ref[:, :width]):
        value = keep[0] * right_side(at) - strides[0] * value
        first[:, at] = value
        low[0, :, at] = value.astype(jnp.bfloat16)
    for at, value in operate(lambda: low[0]):
        value = keep[1] * first[:, at] - momenta[0] * right_side(at) - strides[1] * value
        second[:, at] = value
        low[1, :, at] = value.astype(jnp.bfloat16)
    for at, value in operate(lambda: low[1]):
        value = (
            strides[0] * right_side(at)
            + weights[0] * first[:, at]
            + weights[1] * second[:, at]
            - weights[2] * value
        )
        low[0, :, at] = value.astype(jnp.bfloat16)
    half = examples // 2
    for g in range(2):
        out_ref[g * half : (g + 1) * half, :] = mxu(
            low[0, g * half : (g + 1) * half, :],
            group_ref[g],
            ((1,), (0,)),
        ).astype(out_ref.dtype)


def block_scores(coords, core, squares, far_squares, rest, started, mine, rows):
    vmem = pl.BlockSpec(memory_space=pltpu.VMEM)
    smem = pl.BlockSpec(memory_space=pltpu.SMEM)
    examples = mine.shape[0]
    width = started.shape[0]
    field = (examples, width)
    return pl.pallas_call(
        functools.partial(solve_kernel, coords),
        in_specs=[smem] + [vmem] * 6,
        out_specs=[vmem, vmem],
        out_shape=[
            jax.ShapeDtypeStruct((examples, examples), jnp.bfloat16),
            jax.ShapeDtypeStruct((width, width), jnp.bfloat16),
        ],
        scratch_shapes=[
            pltpu.VMEM(field, jnp.float32),
            pltpu.VMEM(field, jnp.float32),
            pltpu.VMEM((2,) + field, jnp.bfloat16),
        ],
        input_output_aliases={4: 1},
        compiler_params=pltpu.CompilerParams(vmem_limit_bytes=32 << 20),
        name="solve",
    )(core, squares, far_squares, rest, started, mine, rows)[0]


def shifted(value, axis, shift):
    size = lax.axis_size(axis)
    return lax.ppermute(value, axis, [(i, (i + shift) % size) for i in range(size)])


def shards(activations, out_grads, proj_act, proj_out):
    examples = activations.shape[0] // SEQ
    coords = proj_act.shape[1] * proj_out.shape[1]
    blocks = lax.axis_size(OWNERS)
    side = lax.axis_index("side").astype(jnp.int32).reshape(1)
    by_block = features_of(side, activations, out_grads, proj_act, proj_out, blocks)
    arrived = lax.all_to_all(by_block, OWNERS, 0, 0, tiled=True)
    mine = arrived.reshape(blocks * examples, -1)
    other = shifted(mine, "core", 1)

    core = lax.axis_index("core").astype(jnp.int32).reshape(1)
    own, squares, send = gram_parts(core, mine, other)
    across = lax.ppermute(send, ("side", "pair"), [(0, 3), (3, 0), (1, 2), (2, 1)])
    count = own.shape[0]
    width = coords // blocks
    mine_later, other_later, _ = lax.optimization_barrier((mine, other, send))
    rows = in_order(core, mine_later, other_later, width)
    half = (own + across.astype(jnp.float32)).astype(jnp.bfloat16)
    rest = shifted(half, "core", 1)
    started = spread(core, half, width)
    term = block_scores(coords, core, squares, across[count - 16 :], rest, started, mine, rows)
    terms = lax.all_to_all(term.reshape(blocks, examples, -1), OWNERS, 0, 0, tiled=True)
    scores = jnp.sum(terms.astype(jnp.float32), axis=0)
    return scores * float(examples * lax.axis_size(("side", "pair")))


def solution(mesh):
    split = Mesh(mesh.devices.reshape(2, 2, 4, 4, 2), ALL)
    placed = (P(ALL, None), P(ALL, None), P(), P())
    return jax.shard_map(shards, mesh=split, in_specs=placed, out_specs=P(ALL, None), check_vma=False)
```

```python
import functools

import jax
import jax.numpy as jnp
from jax import lax
from jax.experimental import pallas as pl
from jax.experimental.pallas import tpu as pltpu
from jax.sharding import Mesh
from jax.sharding import PartitionSpec as P

SEQ = 64
ITERS = 4
ALL = ("side", "pair", "blk_0", "blk_1", "core")
OWNERS = ("pair", "blk_0", "blk_1")
TILE = 128
PIECES = 8

damping_rate = 0.5
power_steps = 3
STEP = 256


def mxu(a, b, dims):
    return lax.dot_general(a, b, (dims, ((), ())), preferred_element_type=jnp.float32)


def as_three(row):
    high = row.astype(jnp.bfloat16).astype(jnp.float32)
    rest = row - high
    mid = rest.astype(jnp.bfloat16).astype(jnp.float32)
    low = rest - mid
    turn = lax.broadcasted_iota(jnp.int32, (16, row.shape[1]), 0)
    rows = jnp.where(turn == 0, high, jnp.where(turn == 1, mid, jnp.where(turn == 2, low, 0.0)))
    return rows.astype(jnp.bfloat16)


def feature_kernel(
    side_ref, act_ref, grad_ref, pa_ref, po_ref, out_ref, act_low, grad_low, feats, by_coord
):
    step = pl.program_id(0)
    steps = pl.num_programs(0)
    tokens = act_ref.shape[0]
    rows = pl.ds(pl.multiple_of(step * tokens, tokens), tokens)
    act_low[rows, :] = mxu(act_ref[...], pa_ref[...], ((1,), (0,))).astype(jnp.bfloat16)
    grad_low[rows, :] = mxu(grad_ref[...], po_ref[...], ((1,), (0,))).astype(jnp.bfloat16)
    blocks, examples, width = by_coord.shape
    per = width // grad_low.shape[1]
    cols = grad_low.shape[1]

    def eight(half):
        for e in range(8):
            at = pl.ds((half * 8 + e) * SEQ, SEQ)
            feats[e] = mxu(act_low[at, :], grad_low[at, :], ((0,), (0,)))
        turned = jnp.swapaxes(feats[...], 0, 1)
        turned = turned.reshape(blocks, per, 8, cols)
        for j in range(per):
            by_coord[:, half * 8 : half * 8 + 8, j * cols : (j + 1) * cols] = turned[:, j]

    @pl.when(step == steps // 2)
    def _():
        eight(0)

    @pl.when(step == steps - 1)
    def _():
        eight(1)
        acc = jnp.zeros((examples, width), jnp.float32)
        turn = side_ref[0] * (blocks // 2)
        for k in range(blocks):
            low = by_coord[k].astype(jnp.bfloat16)
            out_ref[lax.rem(k + turn, blocks), :, :width] = low
            wide = low.astype(jnp.float32)
            acc = acc + wide * wide
        part = jnp.zeros((8, TILE), jnp.float32)
        for r in range(0, examples, 8):
            for c in range(0, width, TILE):
                part = part + acc[r : r + 8, c : c + TILE]
        tail = as_three(jnp.sum(part, axis=0, keepdims=True))
        for k in range(blocks):
            out_ref[k, :, width:] = tail


def features_of(side, activations, out_grads, proj_act, proj_out, blocks):
    arguments = (activations, out_grads, proj_act, proj_out)
    tokens, depth = activations.shape
    examples = tokens // SEQ
    ra, rb = proj_act.shape[1], proj_out.shape[1]
    width = ra * rb // blocks
    steps = 2
    size = tokens // steps
    return pl.pallas_call(
        feature_kernel,
        grid=(steps,),
        in_specs=[
            pl.BlockSpec(memory_space=pltpu.SMEM),
            pl.BlockSpec((size, depth), lambda i: (i, 0)),
            pl.BlockSpec((size, depth), lambda i: (i, 0)),
            pl.BlockSpec((depth, ra), lambda i: (0, 0), pipeline_mode=pl.Buffered(1)),
            pl.BlockSpec((depth, rb), lambda i: (0, 0), pipeline_mode=pl.Buffered(1)),
        ],
        out_specs=pl.BlockSpec((blocks, examples, width + TILE), lambda i: (0, 0, 0)),
        out_shape=jax.ShapeDtypeStruct((blocks, examples, width + TILE), jnp.bfloat16),
        scratch_shapes=[
            pltpu.VMEM((tokens, ra), jnp.bfloat16),
            pltpu.VMEM((tokens, rb), jnp.bfloat16),
            pltpu.VMEM((8, ra, rb), jnp.float32),
            pltpu.VMEM((blocks, examples, width), jnp.float32),
        ],
        compiler_params=pltpu.CompilerParams(
            dimension_semantics=("arbitrary",), vmem_limit_bytes=32 << 20
        ),
        name="features",
    )(side, *(pltpu.with_memory_space_constraint(x, pltpu.HBM) for x in arguments))


NEAR = ((0, 1), (0, 2), (0, 3), (1, 2), (1, 3))


def row_and_column(size=TILE):
    shape = (size, size)
    return lax.broadcasted_iota(jnp.int32, shape, 0), lax.broadcasted_iota(jnp.int32, shape, 1)


def tile_at(index, count=1):
    if isinstance(index, int):
        return slice(index * TILE, (index + count) * TILE)
    return pl.ds(pl.multiple_of(index * TILE, TILE), count * TILE)


def gram_products(core, rows_ref):
    def product(left, right):
        return mxu(rows_ref[:, left], rows_ref[:, right], ((0,), (0,)))

    for n in range(2):
        first = 4 * core + 2 * n
        left = tile_at(first, 2)
        yield n, 0, product(left, left)
        yield n, 1, product(left, tile_at(lax.rem(first + 2, 8), 2))
        yield n, 2, product(tile_at(2 * n + core), tile_at(2 * n + 4, 2))


def part_of(n, m):
    first = (5 * n + 2 * m) * TILE
    return slice(first, first + (TILE if m == 2 else 2 * TILE))


def own_gram_kernel(core_ref, mine_ref, acc_ref):
    for n, m, value in gram_products(core_ref[0], mine_ref):
        acc_ref[part_of(n, m), :] = value


def gram_kernel(
    core_ref, acc_ref, mine_sum_ref, other_ref, own_a_ref, own_b_ref, sum_ref, send_a_ref, send_b_ref
):
    width = other_ref.shape[1] - TILE
    squares = jnp.sum(
        mine_sum_ref[...].astype(jnp.float32) + other_ref[:, width:].astype(jnp.float32),
        axis=0,
        keepdims=True,
    )
    sum_ref[...] = jnp.broadcast_to(squares, sum_ref.shape)
    row, column = row_and_column()
    parts = {}
    for n, m, value in gram_products(core_ref[0], other_ref):
        parts[n, m] = acc_ref[part_of(n, m), :] + value
    for n, (own_ref, send_ref) in enumerate(((own_a_ref, send_a_ref), (own_b_ref, send_b_ref))):
        near, after, far = parts[n, 0], parts[n, 1], parts[n, 2]
        packed = jnp.where(row <= column, near[:TILE, :TILE], near[TILE:, TILE:])
        inner = jnp.where(row == column, near[TILE:, TILE:], 0.0)
        diagonal = jnp.sum(inner, axis=0, keepdims=True)
        pieces = (
            packed,
            near[:TILE, TILE:],
            after[:TILE, :TILE],
            after[:TILE, TILE:],
            after[TILE:, :TILE],
            after[TILE:, TILE:],
            far[:, :TILE],
            far[:, TILE:],
        )
        for m, piece in enumerate(pieces):
            own_ref[tile_at(m), :] = piece
            send_ref[tile_at(m), :] = piece.astype(jnp.bfloat16)
        turn = lax.broadcasted_iota(jnp.int32, (16, TILE), 0)
        last = jnp.where(turn == 3, diagonal, 0.0)
        rows = slice(PIECES * TILE, PIECES * TILE + 16)
        own_ref[rows, :] = last
        send_ref[rows, :] = as_three(squares) + last.astype(jnp.bfloat16)


def gram_parts(core, mine, other):
    count = PIECES * TILE + 16
    vmem = pl.BlockSpec(memory_space=pltpu.VMEM)
    smem = pl.BlockSpec(memory_space=pltpu.SMEM)
    params = pltpu.CompilerParams(vmem_limit_bytes=16 << 20)
    acc = pl.pallas_call(
        own_gram_kernel,
        in_specs=[smem, vmem],
        out_specs=vmem,
        out_shape=jax.ShapeDtypeStruct((10 * TILE, 2 * TILE), jnp.float32),
        compiler_params=params,
        name="own_gram",
    )(core, mine)
    return pl.pallas_call(
        gram_kernel,
        in_specs=[smem, vmem, vmem, vmem],
        out_specs=[vmem] * 5,
        out_shape=[
            jax.ShapeDtypeStruct((count, TILE), jnp.float32),
            jax.ShapeDtypeStruct((count, TILE), jnp.float32),
            jax.ShapeDtypeStruct((8, TILE), jnp.float32),
            jax.ShapeDtypeStruct((count, TILE), jnp.bfloat16),
            jax.ShapeDtypeStruct((count, TILE), jnp.bfloat16),
        ],
        compiler_params=params,
        name="gram_parts",
    )(core, acc, mine[:, mine.shape[1] - TILE :], other)


def put_pieces(half, n, ref, gram):
    row, column = row_and_column()
    last = ref[PIECES * TILE :, :].astype(jnp.float32)
    first = 4 * half + 2 * n
    packed = ref[tile_at(0), :].astype(jnp.float32)
    turned = packed.T
    upper = jnp.where(row <= column, packed, turned)
    inner = jnp.where(row < column, turned, last[3:4, :])
    lower = jnp.where(row > column, packed, inner)
    gram[tile_at(first), tile_at(first)] = upper.astype(jnp.bfloat16)
    gram[tile_at(first + 1), tile_at(first + 1)] = lower.astype(jnp.bfloat16)
    spots = [(lax.rem(first + i, 8), lax.rem(first + j, 8)) for i, j in NEAR]
    spots += [(2 * n + half, 2 * n + 4), (2 * n + half, 2 * n + 5)]
    for m, (i, j) in enumerate(spots):
        piece = ref[tile_at(1 + m), :]
        gram[tile_at(i), tile_at(j)] = piece
        gram[tile_at(j), tile_at(i)] = piece.T


def spread_kernel(core_ref, half_ref, rest_ref, gram_ref):
    put_pieces(core_ref[0], 0, half_ref, gram_ref)
    put_pieces(1 - core_ref[0], 0, rest_ref, gram_ref)


def spread(core, half, rest, width):
    vmem = pl.BlockSpec(memory_space=pltpu.VMEM)
    return pl.pallas_call(
        spread_kernel,
        in_specs=[pl.BlockSpec(memory_space=pltpu.SMEM), vmem, vmem],
        out_specs=vmem,
        out_shape=jax.ShapeDtypeStruct((width, width), jnp.bfloat16),
        compiler_params=pltpu.CompilerParams(vmem_limit_bytes=16 << 20),
        name="spread",
    )(core, half, rest)


def spread_on_kernel(core_ref, half_ref, started_ref, gram_ref):
    put_pieces(core_ref[0], 1, half_ref, gram_ref)


def spread_on(core, half, started):
    vmem = pl.BlockSpec(memory_space=pltpu.VMEM)
    return pl.pallas_call(
        spread_on_kernel,
        in_specs=[pl.BlockSpec(memory_space=pltpu.SMEM), vmem, vmem],
        out_specs=vmem,
        out_shape=jax.ShapeDtypeStruct(started.shape, jnp.bfloat16),
        input_output_aliases={2: 0},
        compiler_params=pltpu.CompilerParams(vmem_limit_bytes=16 << 20),
        name="spread_on",
    )(core, half, started)


def order_kernel(core_ref, mine_ref, other_ref, out_ref, ordered):
    core = core_ref[0]
    groups, width, examples = out_ref.shape
    piece = 16
    count = examples // (2 * piece)
    for g in range(groups):
        for p in range(count):
            at = slice((g * count + p) * piece, (g * count + p + 1) * piece)
            for which, ref in ((core, mine_ref), (1 - core, other_ref)):
                to = pl.multiple_of(p * 2 * piece + which * piece, piece)
                ordered[g, pl.ds(to, piece), :] = ref[at, :width]
        out_ref[g] = ordered[g].T


def in_order(core, mine, other, width):
    vmem = pl.BlockSpec(memory_space=pltpu.VMEM)
    examples = mine.shape[0]
    return pl.pallas_call(
        order_kernel,
        in_specs=[pl.BlockSpec(memory_space=pltpu.SMEM), vmem, vmem],
        out_specs=vmem,
        out_shape=jax.ShapeDtypeStruct((2, width, examples), jnp.bfloat16),
        scratch_shapes=[pltpu.VMEM((2, examples, width), jnp.bfloat16)],
        compiler_params=pltpu.CompilerParams(vmem_limit_bytes=16 << 20),
        name="in_order",
    )(core, mine, other)


def solve_kernel(
    coords,
    core_ref,
    sum_ref,
    far_sum_ref,
    rest_ref,
    started_ref,
    mine_ref,
    group_ref,
    out_ref,
    gram,
    first,
    second,
    low,
):
    put_pieces(1 - core_ref[0], 1, rest_ref, gram)
    width = gram.shape[0]
    examples = mine_ref.shape[0]
    columns = [slice(c, c + STEP) for c in range(0, width, STEP)]

    def operate(field):
        for at in columns:
            yield at, mxu(field(), gram[:, at], ((1,), (0,)))

    vector = jnp.full((1, width), 1.0 / width**0.5, jnp.float32)
    for _ in range(power_steps):
        image = mxu(as_three(vector), gram[...], ((1,), (0,)))
        image = jnp.sum(image, axis=0, keepdims=True)
        radius = jnp.sqrt(jnp.sum(image * image, axis=1, keepdims=True) + 1e-06)
        vector = image / radius
    total = jnp.sum(sum_ref[0:1, :], axis=1, keepdims=True) + jnp.sum(
        jnp.sum(far_sum_ref[...].astype(jnp.float32)[0:3, :], axis=0, keepdims=True),
        axis=1,
        keepdims=True,
    )
    damping = damping_rate * (total / coords)
    center = damping + radius
    strides = [1.0 / center]
    momenta = []
    for sweep in range(1, ITERS):
        if sweep == 1:
            momenta.append(0.5 * (radius * strides[-1]) ** 2)
        else:
            momenta.append((0.5 * radius * strides[-1]) ** 2)
        strides.append(1.0 / (center - momenta[-1] / strides[-1]))
    keep = [1.0 + m - s * damping for m, s in zip(momenta, strides)]
    weights = (
        strides[1] - strides[3] * momenta[1],
        strides[2] + strides[3] * keep[2],
        strides[3] * strides[2],
    )

    def right_side(at):
        return mine_ref[:, at].astype(jnp.float32)

    for at, value in operate(lambda: mine_ref[:, :width]):
        value = keep[0] * right_side(at) - strides[0] * value
        first[:, at] = value
        low[0, :, at] = value.astype(jnp.bfloat16)
    for at, value in operate(lambda: low[0]):
        value = keep[1] * first[:, at] - momenta[0] * right_side(at) - strides[1] * value
        second[:, at] = value
        low[1, :, at] = value.astype(jnp.bfloat16)
    for at, value in operate(lambda: low[1]):
        value = (
            strides[0] * right_side(at)
            + weights[0] * first[:, at]
            + weights[1] * second[:, at]
            - weights[2] * value
        )
        low[0, :, at] = value.astype(jnp.bfloat16)
    half = examples // 2
    for g in range(2):
        out_ref[g * half : (g + 1) * half, :] = mxu(
            low[0, g * half : (g + 1) * half, :],
            group_ref[g],
            ((1,), (0,)),
        ).astype(out_ref.dtype)


def block_scores(coords, core, squares, far_squares, rest, started, mine, rows):
    vmem = pl.BlockSpec(memory_space=pltpu.VMEM)
    smem = pl.BlockSpec(memory_space=pltpu.SMEM)
    examples = mine.shape[0]
    width = started.shape[0]
    field = (examples, width)
    return pl.pallas_call(
        functools.partial(solve_kernel, coords),
        in_specs=[smem] + [vmem] * 6,
        out_specs=[vmem, vmem],
        out_shape=[
            jax.ShapeDtypeStruct((examples, examples), jnp.bfloat16),
            jax.ShapeDtypeStruct((width, width), jnp.bfloat16),
        ],
        scratch_shapes=[
            pltpu.VMEM(field, jnp.float32),
            pltpu.VMEM(field, jnp.float32),
            pltpu.VMEM((2,) + field, jnp.bfloat16),
        ],
        input_output_aliases={4: 1},
        compiler_params=pltpu.CompilerParams(vmem_limit_bytes=32 << 20),
        name="solve",
    )(core, squares, far_squares, rest, started, mine, rows)[0]


def shifted(value, axis, shift):
    size = lax.axis_size(axis)
    return lax.ppermute(value, axis, [(i, (i + shift) % size) for i in range(size)])


def to_other_owner(value):
    return lax.ppermute(value, ("side", "pair"), [(0, 3), (3, 0), (1, 2), (2, 1)])


def shards(activations, out_grads, proj_act, proj_out):
    examples = activations.shape[0] // SEQ
    coords = proj_act.shape[1] * proj_out.shape[1]
    blocks = lax.axis_size(OWNERS)
    side = lax.axis_index("side").astype(jnp.int32).reshape(1)
    by_block = features_of(side, activations, out_grads, proj_act, proj_out, blocks)
    arrived = lax.all_to_all(by_block, OWNERS, 0, 0, tiled=True)
    mine = arrived.reshape(blocks * examples, -1)
    other = shifted(mine, "core", 1)

    core = lax.axis_index("core").astype(jnp.int32).reshape(1)
    own_a, own_b, squares, send_a, send_b = gram_parts(core, mine, other)
    across_a = to_other_owner(send_a)
    across_b = to_other_owner(send_b)
    width = coords // blocks
    mine_later, other_later, _ = lax.optimization_barrier((mine, other, across_a))
    rows = in_order(core, mine_later, other_later, width)
    half_a = (own_a + across_a.astype(jnp.float32)).astype(jnp.bfloat16)
    rest_a = shifted(half_a, "core", 1)
    started = spread(core, half_a, rest_a, width)
    across_b, rows = lax.optimization_barrier((across_b, rows))
    half_b = (own_b + across_b.astype(jnp.float32)).astype(jnp.bfloat16)
    rest_b = shifted(half_b, "core", 1)
    started = spread_on(core, half_b, started)
    far_squares = across_a[across_a.shape[0] - 16 :]
    term = block_scores(coords, core, squares, far_squares, rest_b, started, mine, rows)
    terms = lax.all_to_all(term.reshape(blocks, examples, -1), OWNERS, 0, 0, tiled=True)
    scores = jnp.sum(terms.astype(jnp.float32), axis=0)
    return scores * float(examples * lax.axis_size(("side", "pair")))


def solution(mesh):
    split = Mesh(mesh.devices.reshape(2, 2, 4, 4, 2), ALL)
    placed = (P(ALL, None), P(ALL, None), P(), P())
    return jax.shard_map(shards, mesh=split, in_specs=placed, out_specs=P(ALL, None), check_vma=False)
```

```python
import functools

import jax
import jax.numpy as jnp
from jax import lax
from jax.experimental import pallas as pl
from jax.experimental.pallas import tpu as pltpu
from jax.sharding import Mesh
from jax.sharding import PartitionSpec as P

SEQ = 64
ITERS = 4
ALL = ("side", "pair", "blk_0", "blk_1", "core")
OWNERS = ("pair", "blk_0", "blk_1")
TILE = 128
PIECES = 8

damping_rate = 0.5
power_steps = 3
STEP = 256


def mxu(a, b, dims):
    return lax.dot_general(a, b, (dims, ((), ())), preferred_element_type=jnp.float32)


def as_three(row):
    high = row.astype(jnp.bfloat16).astype(jnp.float32)
    rest = row - high
    mid = rest.astype(jnp.bfloat16).astype(jnp.float32)
    low = rest - mid
    turn = lax.broadcasted_iota(jnp.int32, (16, row.shape[1]), 0)
    rows = jnp.where(turn == 0, high, jnp.where(turn == 1, mid, jnp.where(turn == 2, low, 0.0)))
    return rows.astype(jnp.bfloat16)


def feature_kernel(
    side_ref, act_ref, grad_ref, pa_ref, po_ref, out_ref, sum_ref, act_low, grad_low, feats, by_coord
):
    step = pl.program_id(0)
    steps = pl.num_programs(0)
    tokens = act_ref.shape[0]
    rows = pl.ds(pl.multiple_of(step * tokens, tokens), tokens)
    act_low[rows, :] = mxu(act_ref[...], pa_ref[...], ((1,), (0,))).astype(jnp.bfloat16)
    grad_low[rows, :] = mxu(grad_ref[...], po_ref[...], ((1,), (0,))).astype(jnp.bfloat16)
    blocks, examples, width = by_coord.shape
    per = width // grad_low.shape[1]
    cols = grad_low.shape[1]

    def eight(half):
        for e in range(8):
            at = pl.ds((half * 8 + e) * SEQ, SEQ)
            feats[e] = mxu(act_low[at, :], grad_low[at, :], ((0,), (0,)))
        turned = jnp.swapaxes(feats[...], 0, 1)
        turned = turned.reshape(blocks, per, 8, cols)
        for j in range(per):
            by_coord[:, half * 8 : half * 8 + 8, j * cols : (j + 1) * cols] = turned[:, j]

    @pl.when(step == steps // 2)
    def _():
        eight(0)

    @pl.when(step == steps - 1)
    def _():
        eight(1)
        acc = jnp.zeros((examples, width), jnp.float32)
        turn = side_ref[0] * (blocks // 2)
        for k in range(blocks):
            low = by_coord[k].astype(jnp.bfloat16)
            out_ref[lax.rem(k + turn, blocks)] = low
            wide = low.astype(jnp.float32)
            acc = acc + wide * wide
        part = jnp.zeros((8, TILE), jnp.float32)
        for r in range(0, examples, 8):
            for c in range(0, width, TILE):
                part = part + acc[r : r + 8, c : c + TILE]
        sum_ref[...] = part


def features_of(side, activations, out_grads, proj_act, proj_out, blocks):
    arguments = (activations, out_grads, proj_act, proj_out)
    tokens, depth = activations.shape
    examples = tokens // SEQ
    ra, rb = proj_act.shape[1], proj_out.shape[1]
    width = ra * rb // blocks
    steps = 2
    size = tokens // steps
    return pl.pallas_call(
        feature_kernel,
        grid=(steps,),
        in_specs=[
            pl.BlockSpec(memory_space=pltpu.SMEM),
            pl.BlockSpec((size, depth), lambda i: (i, 0)),
            pl.BlockSpec((size, depth), lambda i: (i, 0)),
            pl.BlockSpec((depth, ra), lambda i: (0, 0), pipeline_mode=pl.Buffered(1)),
            pl.BlockSpec((depth, rb), lambda i: (0, 0), pipeline_mode=pl.Buffered(1)),
        ],
        out_specs=[
            pl.BlockSpec((blocks, examples, width), lambda i: (0, 0, 0)),
            pl.BlockSpec((8, TILE), lambda i: (0, 0)),
        ],
        out_shape=[
            jax.ShapeDtypeStruct((blocks, examples, width), jnp.bfloat16),
            jax.ShapeDtypeStruct((8, TILE), jnp.float32),
        ],
        scratch_shapes=[
            pltpu.VMEM((tokens, ra), jnp.bfloat16),
            pltpu.VMEM((tokens, rb), jnp.bfloat16),
            pltpu.VMEM((8, ra, rb), jnp.float32),
            pltpu.VMEM((blocks, examples, width), jnp.float32),
        ],
        compiler_params=pltpu.CompilerParams(
            dimension_semantics=("arbitrary",), vmem_limit_bytes=32 << 20
        ),
        name="features",
    )(side, *(pltpu.with_memory_space_constraint(x, pltpu.HBM) for x in arguments))


NEAR = ((0, 1), (0, 2), (0, 3), (1, 2), (1, 3))


def row_and_column(size=TILE):
    shape = (size, size)
    return lax.broadcasted_iota(jnp.int32, shape, 0), lax.broadcasted_iota(jnp.int32, shape, 1)


def tile_at(index, count=1):
    if isinstance(index, int):
        return slice(index * TILE, (index + count) * TILE)
    return pl.ds(pl.multiple_of(index * TILE, TILE), count * TILE)


def gram_products(core, rows_ref):
    def product(left, right):
        return mxu(rows_ref[:, left], rows_ref[:, right], ((0,), (0,)))

    for n in range(2):
        first = 4 * core + 2 * n
        left = tile_at(first, 2)
        yield n, 0, product(left, left)
        yield n, 1, product(left, tile_at(lax.rem(first + 2, 8), 2))
        yield n, 2, product(tile_at(2 * n + core), tile_at(2 * n + 4, 2))


def part_of(n, m):
    first = (5 * n + 2 * m) * TILE
    return slice(first, first + (TILE if m == 2 else 2 * TILE))


def own_gram_kernel(core_ref, mine_ref, acc_ref):
    for n, m, value in gram_products(core_ref[0], mine_ref):
        acc_ref[part_of(n, m), :] = value


def gram_kernel(core_ref, acc_ref, other_ref, own_ref, send_ref):
    row, column = row_and_column()
    parts = {}
    for n, m, value in gram_products(core_ref[0], other_ref):
        parts[n, m] = acc_ref[part_of(n, m), :] + value
    diagonals = []
    for n in range(2):
        near, after, far = parts[n, 0], parts[n, 1], parts[n, 2]
        packed = jnp.where(row <= column, near[:TILE, :TILE], near[TILE:, TILE:])
        inner = jnp.where(row == column, near[TILE:, TILE:], 0.0)
        diagonals.append(jnp.sum(inner, axis=0, keepdims=True))
        pieces = (
            packed,
            near[:TILE, TILE:],
            after[:TILE, :TILE],
            after[:TILE, TILE:],
            after[TILE:, :TILE],
            after[TILE:, TILE:],
            far[:, :TILE],
            far[:, TILE:],
        )
        for m, piece in enumerate(pieces):
            own_ref[tile_at(n * PIECES + m), :] = piece
            send_ref[tile_at(n * PIECES + m), :] = piece.astype(jnp.bfloat16)
    turn = lax.broadcasted_iota(jnp.int32, (16, TILE), 0)
    last = jnp.where(turn == 3, diagonals[0], jnp.where(turn == 4, diagonals[1], 0.0))
    rows = slice(2 * PIECES * TILE, 2 * PIECES * TILE + 16)
    own_ref[rows, :] = last
    send_ref[rows, :] = last.astype(jnp.bfloat16)


def gram_parts(core, mine, other):
    count = 2 * PIECES * TILE + 16
    vmem = pl.BlockSpec(memory_space=pltpu.VMEM)
    smem = pl.BlockSpec(memory_space=pltpu.SMEM)
    params = pltpu.CompilerParams(vmem_limit_bytes=16 << 20)
    acc = pl.pallas_call(
        own_gram_kernel,
        in_specs=[smem, vmem],
        out_specs=vmem,
        out_shape=jax.ShapeDtypeStruct((10 * TILE, 2 * TILE), jnp.float32),
        compiler_params=params,
        name="own_gram",
    )(core, mine)
    return pl.pallas_call(
        gram_kernel,
        in_specs=[smem, vmem, vmem],
        out_specs=[vmem, vmem],
        out_shape=[
            jax.ShapeDtypeStruct((count, TILE), jnp.float32),
            jax.ShapeDtypeStruct((count, TILE), jnp.bfloat16),
        ],
        compiler_params=params,
        name="gram_parts",
    )(core, acc, other)


def put_pieces(half, ref, gram):
    row, column = row_and_column()
    last = ref[2 * PIECES * TILE :, :].astype(jnp.float32)
    for n in range(2):
        first = 4 * half + 2 * n
        packed = ref[tile_at(n * PIECES), :].astype(jnp.float32)
        turned = packed.T
        upper = jnp.where(row <= column, packed, turned)
        inner = jnp.where(row < column, turned, last[3 + n : 4 + n, :])
        lower = jnp.where(row > column, packed, inner)
        gram[tile_at(first), tile_at(first)] = upper.astype(jnp.bfloat16)
        gram[tile_at(first + 1), tile_at(first + 1)] = lower.astype(jnp.bfloat16)
        spots = [(lax.rem(first + i, 8), lax.rem(first + j, 8)) for i, j in NEAR]
        spots += [(2 * n + half, 2 * n + 4), (2 * n + half, 2 * n + 5)]
        for m, (i, j) in enumerate(spots):
            piece = ref[tile_at(n * PIECES + 1 + m), :]
            gram[tile_at(i), tile_at(j)] = piece
            gram[tile_at(j), tile_at(i)] = piece.T


def spread_kernel(core_ref, half_ref, gram_ref):
    put_pieces(core_ref[0], half_ref, gram_ref)


def spread(core, half, width):
    return pl.pallas_call(
        spread_kernel,
        in_specs=[pl.BlockSpec(memory_space=pltpu.SMEM), pl.BlockSpec(memory_space=pltpu.VMEM)],
        out_specs=pl.BlockSpec(memory_space=pltpu.VMEM),
        out_shape=jax.ShapeDtypeStruct((width, width), jnp.bfloat16),
        compiler_params=pltpu.CompilerParams(vmem_limit_bytes=16 << 20),
        name="spread",
    )(core, half)


def order_kernel(core_ref, mine_ref, other_ref, out_ref, ordered):
    core = core_ref[0]
    groups, width, examples = out_ref.shape
    piece = 16
    count = examples // (2 * piece)
    for g in range(groups):
        for p in range(count):
            at = slice((g * count + p) * piece, (g * count + p + 1) * piece)
            for which, ref in ((core, mine_ref), (1 - core, other_ref)):
                to = pl.multiple_of(p * 2 * piece + which * piece, piece)
                ordered[g, pl.ds(to, piece), :] = ref[at, :]
        out_ref[g] = ordered[g].T


def in_order(core, mine, other, width):
    vmem = pl.BlockSpec(memory_space=pltpu.VMEM)
    examples = mine.shape[0]
    return pl.pallas_call(
        order_kernel,
        in_specs=[pl.BlockSpec(memory_space=pltpu.SMEM), vmem, vmem],
        out_specs=vmem,
        out_shape=jax.ShapeDtypeStruct((2, width, examples), jnp.bfloat16),
        scratch_shapes=[pltpu.VMEM((2, examples, width), jnp.bfloat16)],
        compiler_params=pltpu.CompilerParams(vmem_limit_bytes=16 << 20),
        name="in_order",
    )(core, mine, other)


def solve_kernel(
    coords,
    core_ref,
    sum_ref,
    rest_ref,
    started_ref,
    mine_ref,
    group_ref,
    out_ref,
    gram,
    first,
    second,
    low,
):
    put_pieces(1 - core_ref[0], rest_ref, gram)
    width = gram.shape[0]
    examples = mine_ref.shape[0]
    columns = [slice(c, c + STEP) for c in range(0, width, STEP)]

    def operate(field):
        for at in columns:
            yield at, mxu(field(), gram[:, at], ((1,), (0,)))

    vector = jnp.full((1, width), 1.0 / width**0.5, jnp.float32)
    for _ in range(power_steps):
        image = mxu(as_three(vector), gram[...], ((1,), (0,)))
        image = jnp.sum(image, axis=0, keepdims=True)
        radius = jnp.sqrt(jnp.sum(image * image, axis=1, keepdims=True) + 1e-06)
        vector = image / radius
    total = jnp.sum(jnp.sum(sum_ref[...], axis=0, keepdims=True), axis=1, keepdims=True)
    damping = damping_rate * (total / coords)
    center = damping + radius
    strides = [1.0 / center]
    momenta = []
    for sweep in range(1, ITERS):
        if sweep == 1:
            momenta.append(0.5 * (radius * strides[-1]) ** 2)
        else:
            momenta.append((0.5 * radius * strides[-1]) ** 2)
        strides.append(1.0 / (center - momenta[-1] / strides[-1]))
    keep = [1.0 + m - s * damping for m, s in zip(momenta, strides)]
    weights = (
        strides[1] - strides[3] * momenta[1],
        strides[2] + strides[3] * keep[2],
        strides[3] * strides[2],
    )

    def right_side(at):
        return mine_ref[:, at].astype(jnp.float32)

    for at, value in operate(lambda: mine_ref[...]):
        value = keep[0] * right_side(at) - strides[0] * value
        first[:, at] = value
        low[0, :, at] = value.astype(jnp.bfloat16)
    for at, value in operate(lambda: low[0]):
        value = keep[1] * first[:, at] - momenta[0] * right_side(at) - strides[1] * value
        second[:, at] = value
        low[1, :, at] = value.astype(jnp.bfloat16)
    for at, value in operate(lambda: low[1]):
        value = (
            strides[0] * right_side(at)
            + weights[0] * first[:, at]
            + weights[1] * second[:, at]
            - weights[2] * value
        )
        low[0, :, at] = value.astype(jnp.bfloat16)
    half = examples // 2
    for g in range(2):
        out_ref[g * half : (g + 1) * half, :] = mxu(
            low[0, g * half : (g + 1) * half, :],
            group_ref[g],
            ((1,), (0,)),
        ).astype(out_ref.dtype)


def block_scores(coords, core, squares, rest, started, mine, rows):
    vmem = pl.BlockSpec(memory_space=pltpu.VMEM)
    smem = pl.BlockSpec(memory_space=pltpu.SMEM)
    examples = mine.shape[0]
    width = started.shape[0]
    field = (examples, width)
    return pl.pallas_call(
        functools.partial(solve_kernel, coords),
        in_specs=[smem] + [vmem] * 5,
        out_specs=[vmem, vmem],
        out_shape=[
            jax.ShapeDtypeStruct((examples, examples), jnp.bfloat16),
            jax.ShapeDtypeStruct((width, width), jnp.bfloat16),
        ],
        scratch_shapes=[
            pltpu.VMEM(field, jnp.float32),
            pltpu.VMEM(field, jnp.float32),
            pltpu.VMEM((2,) + field, jnp.bfloat16),
        ],
        input_output_aliases={3: 1},
        compiler_params=pltpu.CompilerParams(vmem_limit_bytes=32 << 20),
        name="solve",
    )(core, squares, rest, started, mine, rows)[0]


def shifted(value, axis, shift):
    size = lax.axis_size(axis)
    return lax.ppermute(value, axis, [(i, (i + shift) % size) for i in range(size)])


def to_other_owner(value):
    return lax.ppermute(value, ("side", "pair"), [(0, 3), (3, 0), (1, 2), (2, 1)])


def shards(activations, out_grads, proj_act, proj_out):
    examples = activations.shape[0] // SEQ
    coords = proj_act.shape[1] * proj_out.shape[1]
    blocks = lax.axis_size(OWNERS)
    side = lax.axis_index("side").astype(jnp.int32).reshape(1)
    by_block, squares = features_of(side, activations, out_grads, proj_act, proj_out, blocks)
    arrived = lax.all_to_all(by_block, OWNERS, 0, 0, tiled=True)
    mine = arrived.reshape(blocks * examples, -1)
    other = shifted(mine, "core", 1)

    core = lax.axis_index("core").astype(jnp.int32).reshape(1)
    own, send = gram_parts(core, mine, other)
    squares = squares + to_other_owner(squares)
    squares, send, mine_later, other_later = lax.optimization_barrier(
        (squares, send, mine, other)
    )
    across = to_other_owner(send)
    width = coords // blocks
    squares = jnp.broadcast_to(squares, (blocks,) + squares.shape)
    squares = lax.all_to_all(squares, OWNERS, 0, 0, tiled=True)
    across, squares = lax.optimization_barrier((across, squares))
    rows = in_order(core, mine_later, other_later, width)
    half = (own + across.astype(jnp.float32)).astype(jnp.bfloat16)
    squares = jnp.sum(squares, axis=0)
    rest = shifted(half, "core", 1)
    squares = squares + shifted(squares, "core", 1)
    started = spread(core, half, width)
    term = block_scores(coords, core, squares, rest, started, mine, rows)
    terms = lax.all_to_all(term.reshape(blocks, examples, -1), OWNERS, 0, 0, tiled=True)
    scores = jnp.sum(terms.astype(jnp.float32), axis=0)
    return scores * float(examples * lax.axis_size(("side", "pair")))


def solution(mesh):
    split = Mesh(mesh.devices.reshape(2, 2, 4, 4, 2), ALL)
    placed = (P(ALL, None), P(ALL, None), P(), P())
    return jax.shard_map(shards, mesh=split, in_specs=placed, out_specs=P(ALL, None), check_vma=False)
```

```python
import functools

import jax
import jax.numpy as jnp
from jax import lax
from jax.experimental import pallas as pl
from jax.experimental.pallas import tpu as pltpu
from jax.sharding import Mesh
from jax.sharding import PartitionSpec as P

SEQ = 64
ITERS = 4
ALL = ("side", "pair", "blk_0", "blk_1", "core")
OWNERS = ("pair", "blk_0", "blk_1")
TILE = 128
PIECES = 8

damping_rate = 0.5
power_steps = 3
STEP = 256


def mxu(a, b, dims):
    return lax.dot_general(a, b, (dims, ((), ())), preferred_element_type=jnp.float32)


def as_three(row):
    high = row.astype(jnp.bfloat16).astype(jnp.float32)
    rest = row - high
    mid = rest.astype(jnp.bfloat16).astype(jnp.float32)
    low = rest - mid
    turn = lax.broadcasted_iota(jnp.int32, (16, row.shape[1]), 0)
    rows = jnp.where(turn == 0, high, jnp.where(turn == 1, mid, jnp.where(turn == 2, low, 0.0)))
    return rows.astype(jnp.bfloat16)


def feature_kernel(
    side_ref, act_ref, grad_ref, pa_ref, po_ref, out_ref, sum_ref, act_low, grad_low, feats, by_coord
):
    step = pl.program_id(0)
    steps = pl.num_programs(0)
    tokens = act_ref.shape[0]
    rows = pl.ds(pl.multiple_of(step * tokens, tokens), tokens)
    act_low[rows, :] = mxu(act_ref[...], pa_ref[...], ((1,), (0,))).astype(jnp.bfloat16)
    grad_low[rows, :] = mxu(grad_ref[...], po_ref[...], ((1,), (0,))).astype(jnp.bfloat16)
    blocks, examples, width = by_coord.shape
    per = width // grad_low.shape[1]
    cols = grad_low.shape[1]

    def eight(half):
        for e in range(8):
            at = pl.ds((half * 8 + e) * SEQ, SEQ)
            feats[e] = mxu(act_low[at, :], grad_low[at, :], ((0,), (0,)))
        turned = jnp.swapaxes(feats[...], 0, 1)
        turned = turned.reshape(blocks, per, 8, cols)
        for j in range(per):
            by_coord[:, half * 8 : half * 8 + 8, j * cols : (j + 1) * cols] = turned[:, j]

    @pl.when(step == steps // 2)
    def _():
        eight(0)

    @pl.when(step == steps - 1)
    def _():
        eight(1)
        acc = jnp.zeros((examples, width), jnp.float32)
        turn = side_ref[0] * (blocks // 2)
        for k in range(blocks):
            low = by_coord[k].astype(jnp.bfloat16)
            out_ref[lax.rem(k + turn, blocks)] = low
            wide = low.astype(jnp.float32)
            acc = acc + wide * wide
        part = jnp.zeros((8, TILE), jnp.float32)
        for r in range(0, examples, 8):
            for c in range(0, width, TILE):
                part = part + acc[r : r + 8, c : c + TILE]
        sum_ref[...] = part


def features_of(side, activations, out_grads, proj_act, proj_out, blocks):
    arguments = (activations, out_grads, proj_act, proj_out)
    tokens, depth = activations.shape
    examples = tokens // SEQ
    ra, rb = proj_act.shape[1], proj_out.shape[1]
    width = ra * rb // blocks
    steps = 2
    size = tokens // steps
    return pl.pallas_call(
        feature_kernel,
        grid=(steps,),
        in_specs=[
            pl.BlockSpec(memory_space=pltpu.SMEM),
            pl.BlockSpec((size, depth), lambda i: (i, 0)),
            pl.BlockSpec((size, depth), lambda i: (i, 0)),
            pl.BlockSpec((depth, ra), lambda i: (0, 0), pipeline_mode=pl.Buffered(1)),
            pl.BlockSpec((depth, rb), lambda i: (0, 0), pipeline_mode=pl.Buffered(1)),
        ],
        out_specs=[
            pl.BlockSpec((blocks, examples, width), lambda i: (0, 0, 0)),
            pl.BlockSpec((8, TILE), lambda i: (0, 0)),
        ],
        out_shape=[
            jax.ShapeDtypeStruct((blocks, examples, width), jnp.bfloat16),
            jax.ShapeDtypeStruct((8, TILE), jnp.float32),
        ],
        scratch_shapes=[
            pltpu.VMEM((tokens, ra), jnp.bfloat16),
            pltpu.VMEM((tokens, rb), jnp.bfloat16),
            pltpu.VMEM((8, ra, rb), jnp.float32),
            pltpu.VMEM((blocks, examples, width), jnp.float32),
        ],
        compiler_params=pltpu.CompilerParams(
            dimension_semantics=("arbitrary",), vmem_limit_bytes=32 << 20
        ),
        name="features",
    )(side, *(pltpu.with_memory_space_constraint(x, pltpu.HBM) for x in arguments))


NEAR = ((0, 1), (0, 2), (0, 3), (1, 2), (1, 3))


def row_and_column(size=TILE):
    shape = (size, size)
    return lax.broadcasted_iota(jnp.int32, shape, 0), lax.broadcasted_iota(jnp.int32, shape, 1)


def tile_at(index, count=1):
    if isinstance(index, int):
        return slice(index * TILE, (index + count) * TILE)
    return pl.ds(pl.multiple_of(index * TILE, TILE), count * TILE)


def gram_products(core, rows_ref):
    def product(left, right):
        return mxu(rows_ref[:, left], rows_ref[:, right], ((0,), (0,)))

    for n in range(2):
        first = 4 * core + 2 * n
        left = tile_at(first, 2)
        yield n, 0, product(left, left)
        yield n, 1, product(left, tile_at(lax.rem(first + 2, 8), 2))
        yield n, 2, product(tile_at(2 * n + core), tile_at(2 * n + 4, 2))


def part_of(n, m):
    first = (5 * n + 2 * m) * TILE
    return slice(first, first + (TILE if m == 2 else 2 * TILE))


def own_gram_kernel(core_ref, mine_ref, acc_ref):
    for n, m, value in gram_products(core_ref[0], mine_ref):
        acc_ref[part_of(n, m), :] = value


def gram_kernel(core_ref, acc_ref, other_ref, own_ref, send_ref):
    row, column = row_and_column()
    parts = {}
    for n, m, value in gram_products(core_ref[0], other_ref):
        parts[n, m] = acc_ref[part_of(n, m), :] + value
    diagonals = []
    for n in range(2):
        near, after, far = parts[n, 0], parts[n, 1], parts[n, 2]
        packed = jnp.where(row <= column, near[:TILE, :TILE], near[TILE:, TILE:])
        inner = jnp.where(row == column, near[TILE:, TILE:], 0.0)
        diagonals.append(jnp.sum(inner, axis=0, keepdims=True))
        pieces = (
            packed,
            near[:TILE, TILE:],
            after[:TILE, :TILE],
            after[:TILE, TILE:],
            after[TILE:, :TILE],
            after[TILE:, TILE:],
            far[:, :TILE],
            far[:, TILE:],
        )
        for m, piece in enumerate(pieces):
            own_ref[tile_at(n * PIECES + m), :] = piece
            send_ref[tile_at(n * PIECES + m), :] = piece.astype(jnp.bfloat16)
    turn = lax.broadcasted_iota(jnp.int32, (16, TILE), 0)
    last = jnp.where(turn == 3, diagonals[0], jnp.where(turn == 4, diagonals[1], 0.0))
    rows = slice(2 * PIECES * TILE, 2 * PIECES * TILE + 16)
    own_ref[rows, :] = last
    send_ref[rows, :] = last.astype(jnp.bfloat16)


def gram_parts(core, mine, other):
    count = 2 * PIECES * TILE + 16
    vmem = pl.BlockSpec(memory_space=pltpu.VMEM)
    smem = pl.BlockSpec(memory_space=pltpu.SMEM)
    params = pltpu.CompilerParams(vmem_limit_bytes=16 << 20)
    acc = pl.pallas_call(
        own_gram_kernel,
        in_specs=[smem, vmem],
        out_specs=vmem,
        out_shape=jax.ShapeDtypeStruct((10 * TILE, 2 * TILE), jnp.float32),
        compiler_params=params,
        name="own_gram",
    )(core, mine)
    return pl.pallas_call(
        gram_kernel,
        in_specs=[smem, vmem, vmem],
        out_specs=[vmem, vmem],
        out_shape=[
            jax.ShapeDtypeStruct((count, TILE), jnp.float32),
            jax.ShapeDtypeStruct((count, TILE), jnp.bfloat16),
        ],
        compiler_params=params,
        name="gram_parts",
    )(core, acc, other)


def put_pieces(half, ref, gram):
    row, column = row_and_column()
    last = ref[2 * PIECES * TILE :, :].astype(jnp.float32)
    for n in range(2):
        first = 4 * half + 2 * n
        packed = ref[tile_at(n * PIECES), :].astype(jnp.float32)
        turned = packed.T
        upper = jnp.where(row <= column, packed, turned)
        inner = jnp.where(row < column, turned, last[3 + n : 4 + n, :])
        lower = jnp.where(row > column, packed, inner)
        gram[tile_at(first), tile_at(first)] = upper.astype(jnp.bfloat16)
        gram[tile_at(first + 1), tile_at(first + 1)] = lower.astype(jnp.bfloat16)
        spots = [(lax.rem(first + i, 8), lax.rem(first + j, 8)) for i, j in NEAR]
        spots += [(2 * n + half, 2 * n + 4), (2 * n + half, 2 * n + 5)]
        for m, (i, j) in enumerate(spots):
            piece = ref[tile_at(n * PIECES + 1 + m), :]
            gram[tile_at(i), tile_at(j)] = piece
            gram[tile_at(j), tile_at(i)] = piece.T


def spread_kernel(core_ref, half_ref, gram_ref):
    put_pieces(core_ref[0], half_ref, gram_ref)


def spread(core, half, width):
    return pl.pallas_call(
        spread_kernel,
        in_specs=[pl.BlockSpec(memory_space=pltpu.SMEM), pl.BlockSpec(memory_space=pltpu.VMEM)],
        out_specs=pl.BlockSpec(memory_space=pltpu.VMEM),
        out_shape=jax.ShapeDtypeStruct((width, width), jnp.bfloat16),
        compiler_params=pltpu.CompilerParams(vmem_limit_bytes=16 << 20),
        name="spread",
    )(core, half)


def order_kernel(core_ref, mine_ref, other_ref, out_ref, ordered):
    core = core_ref[0]
    groups, width, examples = out_ref.shape
    piece = 16
    count = examples // (2 * piece)
    for g in range(groups):
        for p in range(count):
            at = slice((g * count + p) * piece, (g * count + p + 1) * piece)
            for which, ref in ((core, mine_ref), (1 - core, other_ref)):
                to = pl.multiple_of(p * 2 * piece + which * piece, piece)
                ordered[g, pl.ds(to, piece), :] = ref[at, :]
        out_ref[g] = ordered[g].T


def in_order(core, mine, other, width):
    vmem = pl.BlockSpec(memory_space=pltpu.VMEM)
    examples = mine.shape[0]
    return pl.pallas_call(
        order_kernel,
        in_specs=[pl.BlockSpec(memory_space=pltpu.SMEM), vmem, vmem],
        out_specs=vmem,
        out_shape=jax.ShapeDtypeStruct((2, width, examples), jnp.bfloat16),
        scratch_shapes=[pltpu.VMEM((2, examples, width), jnp.bfloat16)],
        compiler_params=pltpu.CompilerParams(vmem_limit_bytes=16 << 20),
        name="in_order",
    )(core, mine, other)


def solve_kernel(
    coords,
    core_ref,
    sum_ref,
    rest_ref,
    started_ref,
    mine_ref,
    group_ref,
    out_ref,
    gram,
    first,
    second,
    low,
):
    put_pieces(1 - core_ref[0], rest_ref, gram)
    width = gram.shape[0]
    examples = mine_ref.shape[0]
    columns = [slice(c, c + STEP) for c in range(0, width, STEP)]

    def operate(field):
        for at in columns:
            yield at, mxu(field(), gram[:, at], ((1,), (0,)))

    vector = jnp.full((1, width), 1.0 / width**0.5, jnp.float32)
    for _ in range(power_steps):
        image = mxu(as_three(vector), gram[...], ((1,), (0,)))
        image = jnp.sum(image, axis=0, keepdims=True)
        radius = jnp.sqrt(jnp.sum(image * image, axis=1, keepdims=True) + 1e-06)
        vector = image / radius
    total = jnp.sum(jnp.sum(sum_ref[...], axis=0, keepdims=True), axis=1, keepdims=True)
    damping = damping_rate * (total / coords)
    center = damping + radius
    strides = [1.0 / center]
    momenta = []
    for sweep in range(1, ITERS):
        if sweep == 1:
            momenta.append(0.5 * (radius * strides[-1]) ** 2)
        else:
            momenta.append((0.5 * radius * strides[-1]) ** 2)
        strides.append(1.0 / (center - momenta[-1] / strides[-1]))
    keep = [1.0 + m - s * damping for m, s in zip(momenta, strides)]
    weights = (
        strides[1] - strides[3] * momenta[1],
        strides[2] + strides[3] * keep[2],
        strides[3] * strides[2],
    )

    def right_side(at):
        return mine_ref[:, at].astype(jnp.float32)

    for at, value in operate(lambda: mine_ref[...]):
        value = keep[0] * right_side(at) - strides[0] * value
        first[:, at] = value
        low[0, :, at] = value.astype(jnp.bfloat16)
    for at, value in operate(lambda: low[0]):
        value = keep[1] * first[:, at] - momenta[0] * right_side(at) - strides[1] * value
        second[:, at] = value
        low[1, :, at] = value.astype(jnp.bfloat16)
    for at, value in operate(lambda: low[1]):
        value = (
            strides[0] * right_side(at)
            + weights[0] * first[:, at]
            + weights[1] * second[:, at]
            - weights[2] * value
        )
        low[0, :, at] = value.astype(jnp.bfloat16)
    half = examples // 2
    for g in range(2):
        out_ref[g * half : (g + 1) * half, :] = mxu(
            low[0, g * half : (g + 1) * half, :],
            group_ref[g],
            ((1,), (0,)),
        ).astype(out_ref.dtype)


def block_scores(coords, core, squares, rest, started, mine, rows):
    vmem = pl.BlockSpec(memory_space=pltpu.VMEM)
    smem = pl.BlockSpec(memory_space=pltpu.SMEM)
    examples = mine.shape[0]
    width = started.shape[0]
    field = (examples, width)
    return pl.pallas_call(
        functools.partial(solve_kernel, coords),
        in_specs=[smem] + [vmem] * 5,
        out_specs=[vmem, vmem],
        out_shape=[
            jax.ShapeDtypeStruct((examples, examples), jnp.bfloat16),
            jax.ShapeDtypeStruct((width, width), jnp.bfloat16),
        ],
        scratch_shapes=[
            pltpu.VMEM(field, jnp.float32),
            pltpu.VMEM(field, jnp.float32),
            pltpu.VMEM((2,) + field, jnp.bfloat16),
        ],
        input_output_aliases={3: 1},
        compiler_params=pltpu.CompilerParams(vmem_limit_bytes=32 << 20),
        name="solve",
    )(core, squares, rest, started, mine, rows)[0]


def shifted(value, axis, shift):
    size = lax.axis_size(axis)
    return lax.ppermute(value, axis, [(i, (i + shift) % size) for i in range(size)])


def to_other_owner(value):
    return lax.ppermute(value, ("side", "pair"), [(0, 3), (3, 0), (1, 2), (2, 1)])


def shards(activations, out_grads, proj_act, proj_out):
    examples = activations.shape[0] // SEQ
    coords = proj_act.shape[1] * proj_out.shape[1]
    blocks = lax.axis_size(OWNERS)
    side = lax.axis_index("side").astype(jnp.int32).reshape(1)
    by_block, squares = features_of(side, activations, out_grads, proj_act, proj_out, blocks)
    arrived = lax.all_to_all(by_block, OWNERS, 0, 0, tiled=True)
    mine = arrived.reshape(blocks * examples, -1)
    other = shifted(mine, "core", 1)

    core = lax.axis_index("core").astype(jnp.int32).reshape(1)
    own, send = gram_parts(core, mine, other)
    squares = squares + shifted(squares, "core", 1)
    squares, send, mine_later, other_later = lax.optimization_barrier(
        (squares, send, mine, other)
    )
    across = to_other_owner(send)
    width = coords // blocks
    squares = jnp.broadcast_to(squares, (blocks,) + squares.shape)
    squares = lax.all_to_all(squares, OWNERS, 0, 0, tiled=True)
    across, squares = lax.optimization_barrier((across, squares))
    rows = in_order(core, mine_later, other_later, width)
    half = (own + across.astype(jnp.float32)).astype(jnp.bfloat16)
    squares = jnp.sum(squares, axis=0)
    rest = shifted(half, "core", 1)
    squares = squares + to_other_owner(squares)
    started = spread(core, half, width)
    term = block_scores(coords, core, squares, rest, started, mine, rows)
    terms = lax.all_to_all(term.reshape(blocks, examples, -1), OWNERS, 0, 0, tiled=True)
    scores = jnp.sum(terms.astype(jnp.float32), axis=0)
    return scores * float(examples * lax.axis_size(("side", "pair")))


def solution(mesh):
    split = Mesh(mesh.devices.reshape(2, 2, 4, 4, 2), ALL)
    placed = (P(ALL, None), P(ALL, None), P(), P())
    return jax.shard_map(shards, mesh=split, in_specs=placed, out_specs=P(ALL, None), check_vma=False)
```

```python
import functools

import jax
import jax.numpy as jnp
from jax import lax
from jax.experimental import pallas as pl
from jax.experimental.pallas import tpu as pltpu
from jax.sharding import Mesh
from jax.sharding import PartitionSpec as P

SEQ = 64
ITERS = 4
ALL = ("side", "pair", "blk_0", "blk_1", "core")
OWNERS = ("pair", "blk_0", "blk_1")
TILE = 128
PIECES = 8

damping_rate = 0.5
power_steps = 3
STEP = 256


def mxu(a, b, dims):
    return lax.dot_general(a, b, (dims, ((), ())), preferred_element_type=jnp.float32)


def as_three(row):
    high = row.astype(jnp.bfloat16).astype(jnp.float32)
    rest = row - high
    mid = rest.astype(jnp.bfloat16).astype(jnp.float32)
    low = rest - mid
    turn = lax.broadcasted_iota(jnp.int32, (16, row.shape[1]), 0)
    rows = jnp.where(turn == 0, high, jnp.where(turn == 1, mid, jnp.where(turn == 2, low, 0.0)))
    return rows.astype(jnp.bfloat16)


def feature_kernel(
    side_ref, act_ref, grad_ref, pa_ref, po_ref, out_ref, act_low, grad_low, feats, by_coord
):
    step = pl.program_id(0)
    steps = pl.num_programs(0)
    tokens = act_ref.shape[0]
    rows = pl.ds(pl.multiple_of(step * tokens, tokens), tokens)
    act_low[rows, :] = mxu(act_ref[...], pa_ref[...], ((1,), (0,))).astype(jnp.bfloat16)
    grad_low[rows, :] = mxu(grad_ref[...], po_ref[...], ((1,), (0,))).astype(jnp.bfloat16)
    blocks, examples, width = by_coord.shape
    per = width // grad_low.shape[1]
    cols = grad_low.shape[1]

    def eight(half):
        for e in range(8):
            at = pl.ds((half * 8 + e) * SEQ, SEQ)
            feats[e] = mxu(act_low[at, :], grad_low[at, :], ((0,), (0,)))
        turned = jnp.swapaxes(feats[...], 0, 1)
        turned = turned.reshape(blocks, per, 8, cols)
        for j in range(per):
            by_coord[:, half * 8 : half * 8 + 8, j * cols : (j + 1) * cols] = turned[:, j]

    @pl.when(step == steps // 2)
    def _():
        eight(0)

    @pl.when(step == steps - 1)
    def _():
        eight(1)
        acc = jnp.zeros((examples, width), jnp.float32)
        turn = side_ref[0] * (blocks // 2)
        for k in range(blocks):
            low = by_coord[k].astype(jnp.bfloat16)
            out_ref[lax.rem(k + turn, blocks), :, :width] = low
            wide = low.astype(jnp.float32)
            acc = acc + wide * wide
        part = jnp.zeros((8, TILE), jnp.float32)
        for r in range(0, examples, 8):
            for c in range(0, width, TILE):
                part = part + acc[r : r + 8, c : c + TILE]
        tail = as_three(jnp.sum(part, axis=0, keepdims=True))
        for k in range(blocks):
            out_ref[k, :, width:] = tail


def features_of(side, activations, out_grads, proj_act, proj_out, blocks):
    arguments = (activations, out_grads, proj_act, proj_out)
    tokens, depth = activations.shape
    examples = tokens // SEQ
    ra, rb = proj_act.shape[1], proj_out.shape[1]
    width = ra * rb // blocks
    steps = 2
    size = tokens // steps
    return pl.pallas_call(
        feature_kernel,
        grid=(steps,),
        in_specs=[
            pl.BlockSpec(memory_space=pltpu.SMEM),
            pl.BlockSpec((size, depth), lambda i: (i, 0)),
            pl.BlockSpec((size, depth), lambda i: (i, 0)),
            pl.BlockSpec((depth, ra), lambda i: (0, 0), pipeline_mode=pl.Buffered(1)),
            pl.BlockSpec((depth, rb), lambda i: (0, 0), pipeline_mode=pl.Buffered(1)),
        ],
        out_specs=pl.BlockSpec((blocks, examples, width + TILE), lambda i: (0, 0, 0)),
        out_shape=jax.ShapeDtypeStruct((blocks, examples, width + TILE), jnp.bfloat16),
        scratch_shapes=[
            pltpu.VMEM((tokens, ra), jnp.bfloat16),
            pltpu.VMEM((tokens, rb), jnp.bfloat16),
            pltpu.VMEM((8, ra, rb), jnp.float32),
            pltpu.VMEM((blocks, examples, width), jnp.float32),
        ],
        compiler_params=pltpu.CompilerParams(
            dimension_semantics=("arbitrary",), vmem_limit_bytes=32 << 20
        ),
        name="features",
    )(side, *(pltpu.with_memory_space_constraint(x, pltpu.HBM) for x in arguments))


NEAR = ((0, 1), (0, 2), (0, 3), (1, 2), (1, 3))


def row_and_column(size=TILE):
    shape = (size, size)
    return lax.broadcasted_iota(jnp.int32, shape, 0), lax.broadcasted_iota(jnp.int32, shape, 1)


def tile_at(index, count=1):
    if isinstance(index, int):
        return slice(index * TILE, (index + count) * TILE)
    return pl.ds(pl.multiple_of(index * TILE, TILE), count * TILE)


def gram_products(core, rows_ref):
    def product(left, right):
        return mxu(rows_ref[:, left], rows_ref[:, right], ((0,), (0,)))

    for n in range(2):
        first = 4 * core + 2 * n
        left = tile_at(first, 2)
        yield n, 0, product(left, left)
        yield n, 1, product(left, tile_at(lax.rem(first + 2, 8), 2))
        yield n, 2, product(tile_at(2 * n + core), tile_at(2 * n + 4, 2))


def part_of(n, m):
    first = (5 * n + 2 * m) * TILE
    return slice(first, first + (TILE if m == 2 else 2 * TILE))


def own_gram_kernel(core_ref, mine_ref, acc_ref):
    for n, m, value in gram_products(core_ref[0], mine_ref):
        acc_ref[part_of(n, m), :] = value


def gram_kernel(
    core_ref, acc_ref, mine_sum_ref, other_ref, own_a_ref, own_b_ref, sum_ref, send_a_ref, send_b_ref
):
    width = other_ref.shape[1] - TILE
    squares = jnp.sum(
        mine_sum_ref[...].astype(jnp.float32) + other_ref[:, width:].astype(jnp.float32),
        axis=0,
        keepdims=True,
    )
    sum_ref[...] = jnp.broadcast_to(squares, sum_ref.shape)
    row, column = row_and_column()
    parts = {}
    for n, m, value in gram_products(core_ref[0], other_ref):
        parts[n, m] = acc_ref[part_of(n, m), :] + value
    for n, (own_ref, send_ref) in enumerate(((own_a_ref, send_a_ref), (own_b_ref, send_b_ref))):
        near, after, far = parts[n, 0], parts[n, 1], parts[n, 2]
        packed = jnp.where(row <= column, near[:TILE, :TILE], near[TILE:, TILE:])
        inner = jnp.where(row == column, near[TILE:, TILE:], 0.0)
        diagonal = jnp.sum(inner, axis=0, keepdims=True)
        pieces = (
            packed,
            near[:TILE, TILE:],
            after[:TILE, :TILE],
            after[:TILE, TILE:],
            after[TILE:, :TILE],
            after[TILE:, TILE:],
            far[:, :TILE],
            far[:, TILE:],
        )
        for m, piece in enumerate(pieces):
            own_ref[tile_at(m), :] = piece
            send_ref[tile_at(m), :] = piece.astype(jnp.bfloat16)
        turn = lax.broadcasted_iota(jnp.int32, (16, TILE), 0)
        last = jnp.where(turn == 3, diagonal, 0.0)
        rows = slice(PIECES * TILE, PIECES * TILE + 16)
        own_ref[rows, :] = last
        send_ref[rows, :] = as_three(squares) + last.astype(jnp.bfloat16)


def gram_parts(core, mine, other):
    count = PIECES * TILE + 16
    vmem = pl.BlockSpec(memory_space=pltpu.VMEM)
    smem = pl.BlockSpec(memory_space=pltpu.SMEM)
    params = pltpu.CompilerParams(vmem_limit_bytes=16 << 20)
    acc = pl.pallas_call(
        own_gram_kernel,
        in_specs=[smem, vmem],
        out_specs=vmem,
        out_shape=jax.ShapeDtypeStruct((10 * TILE, 2 * TILE), jnp.float32),
        compiler_params=params,
        name="own_gram",
    )(core, mine)
    return pl.pallas_call(
        gram_kernel,
        in_specs=[smem, vmem, vmem, vmem],
        out_specs=[vmem] * 5,
        out_shape=[
            jax.ShapeDtypeStruct((count, TILE), jnp.float32),
            jax.ShapeDtypeStruct((count, TILE), jnp.float32),
            jax.ShapeDtypeStruct((8, TILE), jnp.float32),
            jax.ShapeDtypeStruct((count, TILE), jnp.bfloat16),
            jax.ShapeDtypeStruct((count, TILE), jnp.bfloat16),
        ],
        compiler_params=params,
        name="gram_parts",
    )(core, acc, mine[:, mine.shape[1] - TILE :], other)


def put_pieces(half, n, ref, gram):
    row, column = row_and_column()
    last = ref[PIECES * TILE :, :].astype(jnp.float32)
    first = 4 * half + 2 * n
    packed = ref[tile_at(0), :].astype(jnp.float32)
    turned = packed.T
    upper = jnp.where(row <= column, packed, turned)
    inner = jnp.where(row < column, turned, last[3:4, :])
    lower = jnp.where(row > column, packed, inner)
    gram[tile_at(first), tile_at(first)] = upper.astype(jnp.bfloat16)
    gram[tile_at(first + 1), tile_at(first + 1)] = lower.astype(jnp.bfloat16)
    spots = [(lax.rem(first + i, 8), lax.rem(first + j, 8)) for i, j in NEAR]
    spots += [(2 * n + half, 2 * n + 4), (2 * n + half, 2 * n + 5)]
    for m, (i, j) in enumerate(spots):
        piece = ref[tile_at(1 + m), :]
        gram[tile_at(i), tile_at(j)] = piece
        gram[tile_at(j), tile_at(i)] = piece.T


def spread_kernel(core_ref, half_ref, rest_ref, gram_ref):
    put_pieces(core_ref[0], 0, half_ref, gram_ref)
    put_pieces(1 - core_ref[0], 0, rest_ref, gram_ref)


def spread(core, half, rest, width):
    vmem = pl.BlockSpec(memory_space=pltpu.VMEM)
    return pl.pallas_call(
        spread_kernel,
        in_specs=[pl.BlockSpec(memory_space=pltpu.SMEM), vmem, vmem],
        out_specs=vmem,
        out_shape=jax.ShapeDtypeStruct((width, width), jnp.bfloat16),
        compiler_params=pltpu.CompilerParams(vmem_limit_bytes=16 << 20),
        name="spread",
    )(core, half, rest)


def spread_on_kernel(core_ref, half_ref, started_ref, gram_ref):
    put_pieces(core_ref[0], 1, half_ref, gram_ref)


def spread_on(core, half, started):
    vmem = pl.BlockSpec(memory_space=pltpu.VMEM)
    return pl.pallas_call(
        spread_on_kernel,
        in_specs=[pl.BlockSpec(memory_space=pltpu.SMEM), vmem, vmem],
        out_specs=vmem,
        out_shape=jax.ShapeDtypeStruct(started.shape, jnp.bfloat16),
        input_output_aliases={2: 0},
        compiler_params=pltpu.CompilerParams(vmem_limit_bytes=16 << 20),
        name="spread_on",
    )(core, half, started)


def order_kernel(core_ref, mine_ref, other_ref, out_ref, ordered):
    core = core_ref[0]
    groups, width, examples = out_ref.shape
    piece = 16
    count = examples // (2 * piece)
    for g in range(groups):
        for p in range(count):
            at = slice((g * count + p) * piece, (g * count + p + 1) * piece)
            for which, ref in ((core, mine_ref), (1 - core, other_ref)):
                to = pl.multiple_of(p * 2 * piece + which * piece, piece)
                ordered[g, pl.ds(to, piece), :] = ref[at, :width]
        out_ref[g] = ordered[g].T


def in_order(core, mine, other, width):
    vmem = pl.BlockSpec(memory_space=pltpu.VMEM)
    examples = mine.shape[0]
    return pl.pallas_call(
        order_kernel,
        in_specs=[pl.BlockSpec(memory_space=pltpu.SMEM), vmem, vmem],
        out_specs=vmem,
        out_shape=jax.ShapeDtypeStruct((2, width, examples), jnp.bfloat16),
        scratch_shapes=[pltpu.VMEM((2, examples, width), jnp.bfloat16)],
        compiler_params=pltpu.CompilerParams(vmem_limit_bytes=16 << 20),
        name="in_order",
    )(core, mine, other)


def solve_kernel(
    coords,
    core_ref,
    sum_ref,
    far_sum_ref,
    rest_ref,
    started_ref,
    mine_ref,
    group_ref,
    out_ref,
    gram,
    first,
    second,
    low,
):
    put_pieces(1 - core_ref[0], 1, rest_ref, gram)
    width = gram.shape[0]
    examples = mine_ref.shape[0]
    columns = [slice(c, c + STEP) for c in range(0, width, STEP)]

    def operate(field):
        for at in columns:
            yield at, mxu(field(), gram[:, at], ((1,), (0,)))

    def image_of(vector):
        return jnp.sum(mxu(as_three(vector), gram[...], ((1,), (0,))), axis=0, keepdims=True)

    def size_of(image):
        return jnp.sqrt(jnp.sum(image * image, axis=1, keepdims=True) + 1e-06)

    image = image_of(jnp.full((1, width), 1.0 / width**0.5, jnp.float32))
    for _ in range(1, power_steps):
        image = image_of(image) * (1.0 / size_of(image))
    radius = size_of(image)
    total = jnp.sum(sum_ref[0:1, :], axis=1, keepdims=True) + jnp.sum(
        jnp.sum(far_sum_ref[...].astype(jnp.float32)[0:3, :], axis=0, keepdims=True),
        axis=1,
        keepdims=True,
    )
    damping = damping_rate * (total / coords)
    center = damping + radius
    strides = [1.0 / center]
    momenta = []
    for sweep in range(1, ITERS):
        ratio = radius * strides[-1]
        factor = 0.5 if sweep == 1 else 0.25
        momenta.append(factor * ratio * ratio)
        strides.append(1.0 / (center - factor * radius * ratio))
    keep = [1.0 + m - s * damping for m, s in zip(momenta, strides)]
    weights = (
        strides[1] - strides[3] * momenta[1],
        strides[2] + strides[3] * keep[2],
        strides[3] * strides[2],
    )

    def right_side(at):
        return mine_ref[:, at].astype(jnp.float32)

    for at, value in operate(lambda: mine_ref[:, :width]):
        value = keep[0] * right_side(at) - strides[0] * value
        first[:, at] = value
        low[0, :, at] = value.astype(jnp.bfloat16)
    for at, value in operate(lambda: low[0]):
        value = keep[1] * first[:, at] - momenta[0] * right_side(at) - strides[1] * value
        second[:, at] = value
        low[1, :, at] = value.astype(jnp.bfloat16)
    for at, value in operate(lambda: low[1]):
        value = (
            strides[0] * right_side(at)
            + weights[0] * first[:, at]
            + weights[1] * second[:, at]
            - weights[2] * value
        )
        low[0, :, at] = value.astype(jnp.bfloat16)
    half = examples // 2
    for g in range(2):
        out_ref[g * half : (g + 1) * half, :] = mxu(
            low[0, g * half : (g + 1) * half, :],
            group_ref[g],
            ((1,), (0,)),
        ).astype(out_ref.dtype)


def block_scores(coords, core, squares, far_squares, rest, started, mine, rows):
    vmem = pl.BlockSpec(memory_space=pltpu.VMEM)
    smem = pl.BlockSpec(memory_space=pltpu.SMEM)
    examples = mine.shape[0]
    width = started.shape[0]
    field = (examples, width)
    return pl.pallas_call(
        functools.partial(solve_kernel, coords),
        in_specs=[smem] + [vmem] * 6,
        out_specs=[vmem, vmem],
        out_shape=[
            jax.ShapeDtypeStruct((examples, examples), jnp.bfloat16),
            jax.ShapeDtypeStruct((width, width), jnp.bfloat16),
        ],
        scratch_shapes=[
            pltpu.VMEM(field, jnp.float32),
            pltpu.VMEM(field, jnp.float32),
            pltpu.VMEM((2,) + field, jnp.bfloat16),
        ],
        input_output_aliases={4: 1},
        compiler_params=pltpu.CompilerParams(vmem_limit_bytes=32 << 20),
        name="solve",
    )(core, squares, far_squares, rest, started, mine, rows)[0]


def shifted(value, axis, shift):
    size = lax.axis_size(axis)
    return lax.ppermute(value, axis, [(i, (i + shift) % size) for i in range(size)])


def to_other_owner(value):
    return lax.ppermute(value, ("side", "pair"), [(0, 3), (3, 0), (1, 2), (2, 1)])


def shards(activations, out_grads, proj_act, proj_out):
    examples = activations.shape[0] // SEQ
    coords = proj_act.shape[1] * proj_out.shape[1]
    blocks = lax.axis_size(OWNERS)
    side = lax.axis_index("side").astype(jnp.int32).reshape(1)
    by_block = features_of(side, activations, out_grads, proj_act, proj_out, blocks)
    arrived = lax.all_to_all(by_block, OWNERS, 0, 0, tiled=True)
    mine = arrived.reshape(blocks * examples, -1)
    other = shifted(mine, "core", 1)

    core = lax.axis_index("core").astype(jnp.int32).reshape(1)
    own_a, own_b, squares, send_a, send_b = gram_parts(core, mine, other)
    across_a = to_other_owner(send_a)
    across_b = to_other_owner(send_b)
    width = coords // blocks
    mine_later, other_later, _ = lax.optimization_barrier((mine, other, across_a))
    rows = in_order(core, mine_later, other_later, width)
    half_a = (own_a + across_a.astype(jnp.float32)).astype(jnp.bfloat16)
    rest_a = shifted(half_a, "core", 1)
    started = spread(core, half_a, rest_a, width)
    across_b, rows = lax.optimization_barrier((across_b, rows))
    half_b = (own_b + across_b.astype(jnp.float32)).astype(jnp.bfloat16)
    rest_b = shifted(half_b, "core", 1)
    started = spread_on(core, half_b, started)
    far_squares = across_a[across_a.shape[0] - 16 :]
    term = block_scores(coords, core, squares, far_squares, rest_b, started, mine, rows)
    terms = lax.all_to_all(term.reshape(blocks, examples, -1), OWNERS, 0, 0, tiled=True)
    scores = jnp.sum(terms.astype(jnp.float32), axis=0)
    return scores * float(examples * lax.axis_size(("side", "pair")))


def solution(mesh):
    split = Mesh(mesh.devices.reshape(2, 2, 4, 4, 2), ALL)
    placed = (P(ALL, None), P(ALL, None), P(), P())
    return jax.shard_map(shards, mesh=split, in_specs=placed, out_specs=P(ALL, None), check_vma=False)
```

```python
import functools

import jax
import jax.numpy as jnp
from jax import lax
from jax.experimental import pallas as pl
from jax.experimental.pallas import tpu as pltpu
from jax.sharding import Mesh
from jax.sharding import PartitionSpec as P

SEQ = 64
ITERS = 4
ALL = ("side", "pair", "blk_0", "blk_1", "core")
OWNERS = ("pair", "blk_0", "blk_1")
TILE = 128
PIECES = 8

damping_rate = 0.5
power_steps = 3
STEP = 256


def mxu(a, b, dims):
    return lax.dot_general(a, b, (dims, ((), ())), preferred_element_type=jnp.float32)


def as_three(row):
    high = row.astype(jnp.bfloat16).astype(jnp.float32)
    rest = row - high
    mid = rest.astype(jnp.bfloat16).astype(jnp.float32)
    low = rest - mid
    turn = lax.broadcasted_iota(jnp.int32, (16, row.shape[1]), 0)
    rows = jnp.where(turn == 0, high, jnp.where(turn == 1, mid, jnp.where(turn == 2, low, 0.0)))
    return rows.astype(jnp.bfloat16)


def feature_kernel(
    side_ref, act_ref, grad_ref, pa_ref, po_ref, out_ref, act_low, grad_low, feats, by_coord
):
    step = pl.program_id(0)
    steps = pl.num_programs(0)
    tokens = act_ref.shape[0]
    rows = pl.ds(pl.multiple_of(step * tokens, tokens), tokens)
    act_low[rows, :] = mxu(act_ref[...], pa_ref[...], ((1,), (0,))).astype(jnp.bfloat16)
    grad_low[rows, :] = mxu(grad_ref[...], po_ref[...], ((1,), (0,))).astype(jnp.bfloat16)
    blocks, examples, width = by_coord.shape
    per = width // grad_low.shape[1]
    cols = grad_low.shape[1]

    def eight(half):
        for e in range(8):
            at = pl.ds((half * 8 + e) * SEQ, SEQ)
            feats[e] = mxu(act_low[at, :], grad_low[at, :], ((0,), (0,)))
        turned = jnp.swapaxes(feats[...], 0, 1)
        turned = turned.reshape(blocks, per, 8, cols)
        for j in range(per):
            by_coord[:, half * 8 : half * 8 + 8, j * cols : (j + 1) * cols] = turned[:, j]

    @pl.when(step == steps // 2)
    def _():
        eight(0)

    @pl.when(step == steps - 1)
    def _():
        eight(1)
        acc = jnp.zeros((examples, width), jnp.float32)
        turn = side_ref[0] * (blocks // 2)
        for k in range(blocks):
            low = by_coord[k].astype(jnp.bfloat16)
            out_ref[lax.rem(k + turn, blocks), :, :width] = low
            wide = low.astype(jnp.float32)
            acc = acc + wide * wide
        part = jnp.zeros((8, TILE), jnp.float32)
        for r in range(0, examples, 8):
            for c in range(0, width, TILE):
                part = part + acc[r : r + 8, c : c + TILE]
        tail = as_three(jnp.sum(part, axis=0, keepdims=True))
        for k in range(blocks):
            out_ref[k, :, width:] = tail


def features_of(side, activations, out_grads, proj_act, proj_out, blocks):
    arguments = (activations, out_grads, proj_act, proj_out)
    tokens, depth = activations.shape
    examples = tokens // SEQ
    ra, rb = proj_act.shape[1], proj_out.shape[1]
    width = ra * rb // blocks
    steps = 2
    size = tokens // steps
    return pl.pallas_call(
        feature_kernel,
        grid=(steps,),
        in_specs=[
            pl.BlockSpec(memory_space=pltpu.SMEM),
            pl.BlockSpec((size, depth), lambda i: (i, 0)),
            pl.BlockSpec((size, depth), lambda i: (i, 0)),
            pl.BlockSpec((depth, ra), lambda i: (0, 0), pipeline_mode=pl.Buffered(1)),
            pl.BlockSpec((depth, rb), lambda i: (0, 0), pipeline_mode=pl.Buffered(1)),
        ],
        out_specs=pl.BlockSpec((blocks, examples, width + TILE), lambda i: (0, 0, 0)),
        out_shape=jax.ShapeDtypeStruct((blocks, examples, width + TILE), jnp.bfloat16),
        scratch_shapes=[
            pltpu.VMEM((tokens, ra), jnp.bfloat16),
            pltpu.VMEM((tokens, rb), jnp.bfloat16),
            pltpu.VMEM((8, ra, rb), jnp.float32),
            pltpu.VMEM((blocks, examples, width), jnp.float32),
        ],
        compiler_params=pltpu.CompilerParams(
            dimension_semantics=("arbitrary",), vmem_limit_bytes=32 << 20
        ),
        name="features",
    )(side, *(pltpu.with_memory_space_constraint(x, pltpu.HBM) for x in arguments))


NEAR = ((0, 1), (0, 2), (0, 3), (1, 2), (1, 3))


def row_and_column(size=TILE):
    shape = (size, size)
    return lax.broadcasted_iota(jnp.int32, shape, 0), lax.broadcasted_iota(jnp.int32, shape, 1)


def tile_at(index, count=1):
    if isinstance(index, int):
        return slice(index * TILE, (index + count) * TILE)
    return pl.ds(pl.multiple_of(index * TILE, TILE), count * TILE)


def gram_products(core, rows_ref):
    def product(left, right):
        return mxu(rows_ref[:, left], rows_ref[:, right], ((0,), (0,)))

    for n in range(2):
        first = 4 * core + 2 * n
        left = tile_at(first, 2)
        yield n, 0, product(left, left)
        yield n, 1, product(left, tile_at(lax.rem(first + 2, 8), 2))
        yield n, 2, product(tile_at(2 * n + core), tile_at(2 * n + 4, 2))


def part_of(n, m):
    first = (5 * n + 2 * m) * TILE
    return slice(first, first + (TILE if m == 2 else 2 * TILE))


def own_gram_kernel(core_ref, mine_ref, acc_ref):
    for n, m, value in gram_products(core_ref[0], mine_ref):
        acc_ref[part_of(n, m), :] = value


def gram_kernel(
    core_ref, acc_ref, mine_sum_ref, other_ref, own_a_ref, own_b_ref, sum_ref, send_a_ref, send_b_ref
):
    width = other_ref.shape[1] - TILE
    squares = jnp.sum(
        mine_sum_ref[...].astype(jnp.float32) + other_ref[:, width:].astype(jnp.float32),
        axis=0,
        keepdims=True,
    )
    sum_ref[...] = jnp.broadcast_to(squares, sum_ref.shape)
    row, column = row_and_column()
    parts = {}
    for n, m, value in gram_products(core_ref[0], other_ref):
        parts[n, m] = acc_ref[part_of(n, m), :] + value
    for n, (own_ref, send_ref) in enumerate(((own_a_ref, send_a_ref), (own_b_ref, send_b_ref))):
        near, after, far = parts[n, 0], parts[n, 1], parts[n, 2]
        packed = jnp.where(row <= column, near[:TILE, :TILE], near[TILE:, TILE:])
        inner = jnp.where(row == column, near[TILE:, TILE:], 0.0)
        diagonal = jnp.sum(inner, axis=0, keepdims=True)
        pieces = (
            packed,
            near[:TILE, TILE:],
            after[:TILE, :TILE],
            after[:TILE, TILE:],
            after[TILE:, :TILE],
            after[TILE:, TILE:],
            far[:, :TILE],
            far[:, TILE:],
        )
        for m, piece in enumerate(pieces):
            own_ref[tile_at(m), :] = piece
            send_ref[tile_at(m), :] = piece.astype(jnp.bfloat16)
        turn = lax.broadcasted_iota(jnp.int32, (16, TILE), 0)
        last = jnp.where(turn == 3, diagonal, 0.0)
        rows = slice(PIECES * TILE, PIECES * TILE + 16)
        own_ref[rows, :] = last
        send_ref[rows, :] = as_three(squares) + last.astype(jnp.bfloat16)


def gram_parts(core, mine, other):
    count = PIECES * TILE + 16
    vmem = pl.BlockSpec(memory_space=pltpu.VMEM)
    smem = pl.BlockSpec(memory_space=pltpu.SMEM)
    params = pltpu.CompilerParams(vmem_limit_bytes=16 << 20)
    acc = pl.pallas_call(
        own_gram_kernel,
        in_specs=[smem, vmem],
        out_specs=vmem,
        out_shape=jax.ShapeDtypeStruct((10 * TILE, 2 * TILE), jnp.float32),
        compiler_params=params,
        name="own_gram",
    )(core, mine)
    return pl.pallas_call(
        gram_kernel,
        in_specs=[smem, vmem, vmem, vmem],
        out_specs=[vmem] * 5,
        out_shape=[
            jax.ShapeDtypeStruct((count, TILE), jnp.float32),
            jax.ShapeDtypeStruct((count, TILE), jnp.float32),
            jax.ShapeDtypeStruct((8, TILE), jnp.float32),
            jax.ShapeDtypeStruct((count, TILE), jnp.bfloat16),
            jax.ShapeDtypeStruct((count, TILE), jnp.bfloat16),
        ],
        compiler_params=params,
        name="gram_parts",
    )(core, acc, mine[:, mine.shape[1] - TILE :], other)


def put_pieces(half, n, ref, gram):
    row, column = row_and_column()
    last = ref[PIECES * TILE :, :].astype(jnp.float32)
    first = 4 * half + 2 * n
    packed = ref[tile_at(0), :].astype(jnp.float32)
    turned = packed.T
    upper = jnp.where(row <= column, packed, turned)
    inner = jnp.where(row < column, turned, last[3:4, :])
    lower = jnp.where(row > column, packed, inner)
    gram[tile_at(first), tile_at(first)] = upper.astype(jnp.bfloat16)
    gram[tile_at(first + 1), tile_at(first + 1)] = lower.astype(jnp.bfloat16)
    spots = [(lax.rem(first + i, 8), lax.rem(first + j, 8)) for i, j in NEAR]
    spots += [(2 * n + half, 2 * n + 4), (2 * n + half, 2 * n + 5)]
    for m, (i, j) in enumerate(spots):
        piece = ref[tile_at(1 + m), :]
        gram[tile_at(i), tile_at(j)] = piece
        gram[tile_at(j), tile_at(i)] = piece.T


def spread_kernel(core_ref, half_ref, rest_ref, gram_ref):
    put_pieces(core_ref[0], 0, half_ref, gram_ref)
    put_pieces(1 - core_ref[0], 0, rest_ref, gram_ref)


def spread(core, half, rest, width):
    vmem = pl.BlockSpec(memory_space=pltpu.VMEM)
    return pl.pallas_call(
        spread_kernel,
        in_specs=[pl.BlockSpec(memory_space=pltpu.SMEM), vmem, vmem],
        out_specs=vmem,
        out_shape=jax.ShapeDtypeStruct((width, width), jnp.bfloat16),
        compiler_params=pltpu.CompilerParams(vmem_limit_bytes=16 << 20),
        name="spread",
    )(core, half, rest)


def spread_on_kernel(core_ref, half_ref, started_ref, gram_ref):
    put_pieces(core_ref[0], 1, half_ref, gram_ref)


def spread_on(core, half, started):
    vmem = pl.BlockSpec(memory_space=pltpu.VMEM)
    return pl.pallas_call(
        spread_on_kernel,
        in_specs=[pl.BlockSpec(memory_space=pltpu.SMEM), vmem, vmem],
        out_specs=vmem,
        out_shape=jax.ShapeDtypeStruct(started.shape, jnp.bfloat16),
        input_output_aliases={2: 0},
        compiler_params=pltpu.CompilerParams(vmem_limit_bytes=16 << 20),
        name="spread_on",
    )(core, half, started)


def order_kernel(core_ref, mine_ref, other_ref, out_ref, ordered):
    core = core_ref[0]
    groups, width, examples = out_ref.shape
    piece = 16
    count = examples // (2 * piece)
    for g in range(groups):
        for p in range(count):
            at = slice((g * count + p) * piece, (g * count + p + 1) * piece)
            for which, ref in ((core, mine_ref), (1 - core, other_ref)):
                to = pl.multiple_of(p * 2 * piece + which * piece, piece)
                ordered[g, pl.ds(to, piece), :] = ref[at, :width]
        out_ref[g] = ordered[g].T


def in_order(core, mine, other, width):
    vmem = pl.BlockSpec(memory_space=pltpu.VMEM)
    examples = mine.shape[0]
    return pl.pallas_call(
        order_kernel,
        in_specs=[pl.BlockSpec(memory_space=pltpu.SMEM), vmem, vmem],
        out_specs=vmem,
        out_shape=jax.ShapeDtypeStruct((2, width, examples), jnp.bfloat16),
        scratch_shapes=[pltpu.VMEM((2, examples, width), jnp.bfloat16)],
        compiler_params=pltpu.CompilerParams(vmem_limit_bytes=16 << 20),
        name="in_order",
    )(core, mine, other)


def solve_kernel(
    coords,
    scale,
    core_ref,
    sum_ref,
    far_sum_ref,
    rest_ref,
    started_ref,
    mine_ref,
    group_ref,
    out_ref,
    gram,
    first,
    second,
    low,
):
    put_pieces(1 - core_ref[0], 1, rest_ref, gram)
    width = gram.shape[0]
    examples = mine_ref.shape[0]
    columns = [slice(c, c + STEP) for c in range(0, width, STEP)]

    def operate(field):
        for at in columns:
            yield at, mxu(field(), gram[:, at], ((1,), (0,)))

    def image_of(vector):
        return jnp.sum(mxu(as_three(vector), gram[...], ((1,), (0,))), axis=0, keepdims=True)

    def size_of(image):
        return jnp.sqrt(jnp.sum(image * image, axis=1, keepdims=True) + 1e-06)

    image = image_of(jnp.full((1, width), 1.0 / width**0.5, jnp.float32))
    for _ in range(1, power_steps):
        image = image_of(image) * (1.0 / size_of(image))
    radius = size_of(image)
    total = jnp.sum(sum_ref[0:1, :], axis=1, keepdims=True) + jnp.sum(
        jnp.sum(far_sum_ref[...].astype(jnp.float32)[0:3, :], axis=0, keepdims=True),
        axis=1,
        keepdims=True,
    )
    damping = damping_rate * (total / coords)
    center = damping + radius
    strides = [1.0 / center]
    momenta = []
    for sweep in range(1, ITERS):
        ratio = radius * strides[-1]
        factor = 0.5 if sweep == 1 else 0.25
        momenta.append(factor * ratio * ratio)
        strides.append(1.0 / (center - factor * radius * ratio))
    keep = [1.0 + m - s * damping for m, s in zip(momenta, strides)]
    weights = (
        scale * (strides[1] - strides[3] * momenta[1]),
        scale * (strides[2] + strides[3] * keep[2]),
        scale * (strides[3] * strides[2]),
    )
    start = scale * strides[0]

    def right_side(at):
        return mine_ref[:, at].astype(jnp.float32)

    for at, value in operate(lambda: mine_ref[:, :width]):
        value = keep[0] * right_side(at) - strides[0] * value
        first[:, at] = value
        low[0, :, at] = value.astype(jnp.bfloat16)
    for at, value in operate(lambda: low[0]):
        value = keep[1] * first[:, at] - momenta[0] * right_side(at) - strides[1] * value
        second[:, at] = value
        low[1, :, at] = value.astype(jnp.bfloat16)
    for at, value in operate(lambda: low[1]):
        value = (
            start * right_side(at)
            + weights[0] * first[:, at]
            + weights[1] * second[:, at]
            - weights[2] * value
        )
        low[0, :, at] = value.astype(jnp.bfloat16)
    half = examples // 2
    for g in range(2):
        out_ref[g * half : (g + 1) * half, :] = mxu(
            low[0, g * half : (g + 1) * half, :],
            group_ref[g],
            ((1,), (0,)),
        ).astype(out_ref.dtype)


def block_scores(coords, scale, core, squares, far_squares, rest, started, mine, rows):
    vmem = pl.BlockSpec(memory_space=pltpu.VMEM)
    smem = pl.BlockSpec(memory_space=pltpu.SMEM)
    examples = mine.shape[0]
    width = started.shape[0]
    field = (examples, width)
    return pl.pallas_call(
        functools.partial(solve_kernel, coords, scale),
        in_specs=[smem] + [vmem] * 6,
        out_specs=[vmem, vmem],
        out_shape=[
            jax.ShapeDtypeStruct((examples, examples), jnp.bfloat16),
            jax.ShapeDtypeStruct((width, width), jnp.bfloat16),
        ],
        scratch_shapes=[
            pltpu.VMEM(field, jnp.float32),
            pltpu.VMEM(field, jnp.float32),
            pltpu.VMEM((2,) + field, jnp.bfloat16),
        ],
        input_output_aliases={4: 1},
        compiler_params=pltpu.CompilerParams(vmem_limit_bytes=32 << 20),
        name="solve",
    )(core, squares, far_squares, rest, started, mine, rows)[0]


def shifted(value, axis, shift):
    size = lax.axis_size(axis)
    return lax.ppermute(value, axis, [(i, (i + shift) % size) for i in range(size)])


def to_other_owner(value):
    return lax.ppermute(value, ("side", "pair"), [(0, 3), (3, 0), (1, 2), (2, 1)])


def shards(activations, out_grads, proj_act, proj_out):
    examples = activations.shape[0] // SEQ
    coords = proj_act.shape[1] * proj_out.shape[1]
    blocks = lax.axis_size(OWNERS)
    side = lax.axis_index("side").astype(jnp.int32).reshape(1)
    by_block = features_of(side, activations, out_grads, proj_act, proj_out, blocks)
    arrived = lax.all_to_all(by_block, OWNERS, 0, 0, tiled=True)
    mine = arrived.reshape(blocks * examples, -1)
    other = shifted(mine, "core", 1)

    core = lax.axis_index("core").astype(jnp.int32).reshape(1)
    own_a, own_b, squares, send_a, send_b = gram_parts(core, mine, other)
    across_a = to_other_owner(send_a)
    across_b = to_other_owner(send_b)
    width = coords // blocks
    mine_later, other_later, _ = lax.optimization_barrier((mine, other, across_a))
    rows = in_order(core, mine_later, other_later, width)
    half_a = (own_a + across_a.astype(jnp.float32)).astype(jnp.bfloat16)
    rest_a = shifted(half_a, "core", 1)
    started = spread(core, half_a, rest_a, width)
    across_b, rows = lax.optimization_barrier((across_b, rows))
    half_b = (own_b + across_b.astype(jnp.float32)).astype(jnp.bfloat16)
    rest_b = shifted(half_b, "core", 1)
    started = spread_on(core, half_b, started)
    far_squares = across_a[across_a.shape[0] - 16 :]
    scale = float(examples * lax.axis_size(("side", "pair")))
    term = block_scores(coords, scale, core, squares, far_squares, rest_b, started, mine, rows)
    terms = lax.all_to_all(term.reshape(blocks, examples, -1), OWNERS, 0, 0, tiled=True)
    return jnp.sum(terms.astype(jnp.float32), axis=0)


def solution(mesh):
    split = Mesh(mesh.devices.reshape(2, 2, 4, 4, 2), ALL)
    placed = (P(ALL, None), P(ALL, None), P(), P())
    return jax.shard_map(shards, mesh=split, in_specs=placed, out_specs=P(ALL, None), check_vma=False)
```
